512 devices in a mesh: sec: 2 (over core), ctx: 64 (over x, z_hi, y), head: 4 (over z_lo).
Axes of the slice: x: 4, y: 8, z: 8 (z_hi: 2, z_lo: 4; z = z_hi * 4 + z_lo), core: 2. Of those that a mesh axis runs over, the one named last changes fastest.
Arguments:
- query_self: bfloat16 [12288, 2048], P('ctx', ('sec', 'head')), may hold values from -12 to 12
- key_self: bfloat16 [12288, 2048], P('ctx', ('sec', 'head')), may hold values from -6 to 6
- value_self: bfloat16 [12288, 2048], P('ctx', ('sec', 'head')), may hold values from -6 to 6
- query_cross: bfloat16 [12288, 2048], P('ctx', ('sec', 'head')), may hold values from -12 to 12
- neighbour_kv: bfloat16 [512, 128, 4096], P(('sec', 'ctx', 'head')), may hold values from -6 to 6
- neighbour_map: int32 [192, 2], P('ctx'), may hold values from 0 to 7, all different within a row
Outputs:
- self_out: bfloat16 [12288, 2048], P('ctx', ('sec', 'head'))
- cross_out: bfloat16 [12288, 2048], P('ctx', ('sec', 'head'))
The draws below stay inside these ranges and needn't reach their ends.
Inputs may be any that keep to these rules, and one draw needn't show every extreme that they name: `neighbour_map`: entry v of stretch c names slot v % 1 of the device at index v // 1 along sec+head that shares stretch c's context shard; a stretch's two entries differ.
All inputs are finite; a program needn't handle non-finite values.
Results may differ from the reference program's by a relative error of at most 0.0035.
Values may be sent and summed in bfloat16 or wider, within the bound.
No kernel may reach another device: no remote copies, remote signals or barrier semaphores. Data moves between devices by JAX's collectives and lax.ppermute only.
A program may use at most 64 MiB of HBM per device.

```python
import math
import jax
import jax.numpy as jnp
from jax import lax

HD = 128
NH = 16
STRETCH = 64
NB_LEN = 128
NEIGH = 2
SLOTS = 1
SEQ = 12288
STRETCHES = 192
CPD = 3
GROUP = 8
HPD = 2
BLOCKS = 512
N_SEC = 2
N_CTX = 64
N_HEAD = 4


def draw_query_self(key, part):
    inner_key = jax.random.fold_in(key, 1)
    drawn = jnp.clip(3.0 * jax.random.normal(inner_key, (SEQ, NH * HD), jnp.float32), -12.0, 12.0)
    return drawn.astype(jnp.bfloat16)


def draw_key_self(key, part):
    inner_key = jax.random.fold_in(key, 2)
    drawn = jnp.clip(jax.random.normal(inner_key, (SEQ, NH * HD), jnp.float32), -6.0, 6.0)
    return drawn.astype(jnp.bfloat16)


def draw_query_cross(key, part):
    inner_key = jax.random.fold_in(key, 3)
    drawn = jnp.clip(3.0 * jax.random.normal(inner_key, (SEQ, NH * HD), jnp.float32), -12.0, 12.0)
    return drawn.astype(jnp.bfloat16)


def draw_neighbour_kv(key, part):
    inner_key = jax.random.fold_in(key, 4)
    drawn = jnp.clip(jax.random.normal(inner_key, (BLOCKS, NB_LEN, NH * 2 * HD), jnp.float32), -6.0, 6.0)
    return drawn.astype(jnp.bfloat16)


def level_of(key, dims, cuts, low, high):
    loudness = 1.0
    for axis_at, parts in cuts:
        steps = jax.random.uniform(jax.random.fold_in(jax.random.fold_in(key, 6), axis_at), (parts,), jnp.float32, low / len(cuts), high / len(cuts))
        loudness = loudness * jnp.repeat(jnp.exp(steps), dims[axis_at] // parts).reshape((-1,) + (1,) * (len(dims) - 1 - axis_at))
    return loudness


def different_ones(own_key, rows, count, top, lift):
    sequence = jax.random.permutation(jax.random.fold_in(own_key, 1), count)
    pull = sequence
    for power in range(3):
        pull = pull * pull // count
    pull = pull * lift // count
    tickets = jax.random.randint(jax.random.fold_in(own_key, 2), (rows, count), 0, 4096) + pull
    holders = jax.random.permutation(jax.random.fold_in(own_key, 3), rows)[jnp.arange(count) % rows]
    tickets = jnp.where(jnp.arange(rows)[:, None] == holders[None, :], 1 << 14, tickets)
    score = tickets * count + jnp.arange(count)
    return lax.top_k(score.astype(jnp.int32), top)[1].astype(jnp.int32)


def noise(key, shape, scale, limit, shards=(), kind=jnp.bfloat16):
    values = jax.random.normal(key, shape, jnp.float32) * scale
    if len(shards) > 0:
        values = level_of(key, shape, shards, -0.22, 0.18) * values
    return jnp.clip(values, min=-limit, max=limit).astype(kind)


def setup_inputs(seed: int = 0) -> dict:
    arg_keys = jax.random.split(jax.random.key(seed), 7)
    return {
        "query_self": draw_query_self(jax.random.fold_in(arg_keys[6], 71), 0),
        "key_self": draw_key_self(jax.random.fold_in(arg_keys[6], 71), 0),
        "value_self": noise(arg_keys[2], (SEQ, NH * HD), 1.0, 6.0, ((0, 64), (1, 8))),
        "query_cross": draw_query_cross(jax.random.fold_in(arg_keys[6], 71), 0),
        "neighbour_kv": draw_neighbour_kv(jax.random.fold_in(arg_keys[6], 71), 0),
        "neighbour_map": different_ones(arg_keys[5], STRETCHES, N_SEC * N_HEAD * SLOTS, NEIGH, 4096),
    }


MASKED_SCORE = -1e+30

def softmax_attend(scores, key_mask, value_rows):
    masked = jnp.where(key_mask, scores, MASKED_SCORE)
    row_top = lax.optimization_barrier(jnp.max(masked, axis=-1, keepdims=True))
    exp_scores = jnp.where(key_mask, jnp.exp(masked - row_top), 0.0)
    row_total = lax.optimization_barrier(jnp.sum(exp_scores, axis=-1))
    rounded = lax.optimization_barrier(exp_scores.astype(jnp.bfloat16))
    summed = jnp.einsum('hqk,khd->qhd', rounded.astype(jnp.float32), value_rows)
    return summed / jnp.transpose(row_total)[:, :, None]

def reference(query_self, key_self, value_self, query_cross, neighbour_kv, neighbour_map):
    score_scale = 1.0 / math.sqrt(HD)
    query_full = query_self.astype(jnp.float32).reshape(SEQ, NH, HD)
    key_full = key_self.astype(jnp.float32).reshape(SEQ, NH, HD)
    value_full = value_self.astype(jnp.float32).reshape(SEQ, NH, HD)
    block_rows = min(SEQ, 512)
    pieces = []
    for first_row in range(0, SEQ, block_rows):
        last_row = first_row + block_rows
        scores = jnp.einsum('qhd,khd->hqk', query_full[first_row:last_row], key_full[:last_row]) * score_scale
        query_pos = first_row + jnp.arange(block_rows, dtype=jnp.int32)
        key_pos = jnp.arange(last_row, dtype=jnp.int32)
        key_mask = key_pos[None, None, :] <= query_pos[None, :, None]
        pieces.append(softmax_attend(scores, key_mask, value_full[:last_row]))
    self_out = jnp.concatenate(pieces, axis=0).reshape(SEQ, NH * HD).astype(jnp.bfloat16)
    blocks_view = neighbour_kv.reshape(BLOCKS, NB_LEN, GROUP, 2, HPD, HD)
    neighbour_keys = blocks_view[:, :, :, 0].reshape(BLOCKS, NB_LEN, NH, HD)
    neighbour_values = blocks_view[:, :, :, 1].reshape(BLOCKS, NB_LEN, NH, HD)
    stretch_ids = jnp.arange(STRETCHES, dtype=jnp.int32)
    shard_ids = stretch_ids // CPD
    holder = neighbour_map // SLOTS
    position = neighbour_map % SLOTS
    section = holder // N_HEAD
    within = holder % N_HEAD
    block_ids = (((section * N_CTX + shard_ids[:, None]) * N_HEAD + within) * SLOTS + position).astype(jnp.int32)
    stretch_queries = query_cross.reshape(STRETCHES, STRETCH, NH, HD)

    def one_stretch(scanned):
        stretch_query, block_pair, stretch_id = scanned
        key_rows = jnp.take(neighbour_keys, block_pair, axis=0).reshape(NEIGH * NB_LEN, NH, HD).astype(jnp.float32)
        value_rows = jnp.take(neighbour_values, block_pair, axis=0).reshape(NEIGH * NB_LEN, NH, HD).astype(jnp.float32)
        scores = jnp.einsum('qhd,khd->hqk', stretch_query.astype(jnp.float32), key_rows) * score_scale
        key_mask = jnp.ones((1, 1, NEIGH * NB_LEN), dtype=jnp.bool_)
        attended = softmax_attend(scores, key_mask, value_rows)
        return jnp.where(stretch_id > 0, attended, 0.0)
    crossed = lax.map(one_stretch, (stretch_queries, block_ids, stretch_ids))
    cross_out = crossed.reshape(SEQ, NH * HD).astype(jnp.bfloat16)
    return (self_out, cross_out)
```

```python
import functools
import math

import jax
import jax.numpy as jnp
from jax import lax
from jax.experimental import pallas as pl
from jax.experimental.pallas import tpu as pltpu
from jax.sharding import Mesh
from jax.sharding import PartitionSpec as P

HD = 128
STRETCH = 64
NX, NZ, NY = 4, 2, 8
ROWS = 192
WIDTH = 256
STAT_ROWS = 16
KEYS = NX * NZ * ROWS
CHUNK = 256
LOW = -1e30
FAR = 1 << 30
SCALE = 1.0 / math.sqrt(HD)
LOG2E = math.log2(math.e)


def partial_kernel(place_ref, kpos_ref, q_ref, kv0, kv1, kv2, kv3, kv4, kv5, kv6, kv7,
                   out_ref, k_scr, v_scr, s_scr, sem):
    i = pl.program_id(0)
    first = place_ref[0]
    pieces = (kv0, kv1, kv2, kv3, kv4, kv5, kv6, kv7)

    @pl.when(i == 0)
    def _():
        copies = []
        for p, kv in enumerate(pieces):
            copies.append(pltpu.make_async_copy(
                kv.at[pl.ds(0, ROWS), :], k_scr.at[pl.ds(p * ROWS, ROWS), :], sem.at[p, 0]))
            for h in range(2):
                copies.append(pltpu.make_async_copy(
                    kv.at[pl.ds(ROWS, ROWS), pl.ds(h * HD, HD)],
                    v_scr.at[h, pl.ds(p * ROWS, ROWS), pl.ds(0, HD)], sem.at[p, 1 + h]))
        for c in copies:
            c.start()
        v_scr[0, :, HD:] = jnp.ones((KEYS, HD), jnp.bfloat16)
        v_scr[1, :, HD:] = jnp.ones((KEYS, HD), jnp.bfloat16)
        for c in copies:
            c.wait()

    qpos = first + i * ROWS + lax.broadcasted_iota(jnp.int32, (ROWS, CHUNK), 0)
    c2 = SCALE * LOG2E
    for h in range(2):
        qh = q_ref[0, :, h * HD:(h + 1) * HD]
        top = jnp.full((ROWS, HD), LOW, jnp.float32)
        for c in range(KEYS // CHUNK):
            kc = k_scr[pl.ds(c * CHUNK, CHUNK), h * HD:(h + 1) * HD]
            s = lax.dot_general(qh, kc, (((1,), (1,)), ((), ())),
                                preferred_element_type=jnp.float32)
            kp = kpos_ref[0:1, c * CHUNK:(c + 1) * CHUNK]
            s = jnp.where(kp <= qpos, s, LOW)
            s_scr[:, c * CHUNK:(c + 1) * CHUNK] = s
            top = jnp.maximum(top, jnp.maximum(s[:, :HD], s[:, HD:]))
        top = jnp.broadcast_to(jnp.max(top, axis=1, keepdims=True), (ROWS, HD))
        off = jnp.maximum(top, -1e20) * c2
        off2 = jnp.concatenate([off, off], axis=1)
        acc = jnp.zeros((ROWS, 2 * HD), jnp.float32)
        for c in range(KEYS // CHUNK):
            s = s_scr[:, c * CHUNK:(c + 1) * CHUNK]
            p = jnp.exp2(s * c2 - off2).astype(jnp.bfloat16)
            acc = acc + lax.dot_general(p, v_scr[h, pl.ds(c * CHUNK, CHUNK), :],
                                        (((1,), (0,)), ((), ())),
                                        preferred_element_type=jnp.float32)
        total = jnp.maximum(acc[:, HD:], 1e-30)
        out_ref[0, 0:ROWS, h * HD:(h + 1) * HD] = (acc[:, :HD] / total).astype(jnp.bfloat16)
        stat = jnp.where(top > 0.5 * LOW, top * SCALE + jnp.log(total), LOW)
        row = jnp.transpose(stat)[0:STAT_ROWS // 2, :]
        hi = row.astype(jnp.bfloat16).astype(jnp.float32)
        mid = (row - hi).astype(jnp.bfloat16).astype(jnp.float32)
        low = row - hi - mid
        at = lax.broadcasted_iota(jnp.int32, row.shape, 0)
        coded = jnp.where(at == 0, hi, jnp.where(at == 1, mid, low))
        if h == 0:
            held = coded
        else:
            out_ref[0, ROWS:ROWS + STAT_ROWS, 0:ROWS] = jnp.concatenate(
                [held, coded], axis=0).astype(jnp.bfloat16)
    out_ref[0, ROWS:ROWS + STAT_ROWS, ROWS:] = jnp.zeros((STAT_ROWS, WIDTH - ROWS), jnp.bfloat16)


def partial_attention(place, kpos, q_all, pieces):
    whole = pl.BlockSpec(memory_space=pl.ANY)
    return pl.pallas_call(
        partial_kernel,
        out_shape=jax.ShapeDtypeStruct((NY, ROWS + STAT_ROWS, WIDTH), jnp.bfloat16),
        grid=(NY,),
        in_specs=[
            pl.BlockSpec(memory_space=pltpu.SMEM),
            pl.BlockSpec((1, KEYS), lambda i: (0, 0)),
            pl.BlockSpec((1, ROWS, WIDTH), lambda i: (i, 0, 0)),
        ] + [whole] * 8,
        out_specs=pl.BlockSpec((1, ROWS + STAT_ROWS, WIDTH), lambda i: (i, 0, 0)),
        scratch_shapes=[
            pltpu.VMEM((KEYS, WIDTH), jnp.bfloat16),
            pltpu.VMEM((2, KEYS, WIDTH), jnp.bfloat16),
            pltpu.VMEM((ROWS, KEYS), jnp.float32),
            pltpu.SemaphoreType.DMA((8, 3)),
        ],
        cost_estimate=pl.CostEstimate(
            flops=4 * NY * ROWS * KEYS * WIDTH, bytes_accessed=4 * KEYS * WIDTH,
            transcendentals=2 * NY * ROWS * KEYS),
        compiler_params=pltpu.CompilerParams(vmem_limit_bytes=12 << 20),
        name="partial_attention",
    )(place, kpos, q_all, *pieces)


def combine_kernel(part_ref, out_ref):
    stats = []
    for h in range(2):
        rows = []
        for j in range(NY):
            block = part_ref[j, pl.ds(ROWS, STAT_ROWS), :].astype(jnp.float32)
            b = block[8 * h:8 * h + 8]
            rows.append(b[0:1] + b[1:2] + b[2:3])
        top = functools.reduce(jnp.maximum, rows)
        ws = [jnp.exp(r - top) for r in rows]
        inv = 1.0 / functools.reduce(jnp.add, ws)
        stats += [w * inv for w in ws]
    table = jnp.concatenate(stats, axis=0)
    cols = jnp.transpose(table)[0:ROWS]
    for h in range(2):
        acc = jnp.zeros((ROWS, HD), jnp.float32)
        for j in range(NY):
            o = part_ref[j, 0:ROWS, h * HD:(h + 1) * HD].astype(jnp.float32)
            acc = acc + o * cols[:, h * NY + j:h * NY + j + 1]
        out_ref[:, h * HD:(h + 1) * HD] = acc.astype(jnp.bfloat16)


def combine(parts):
    return pl.pallas_call(
        combine_kernel,
        out_shape=jax.ShapeDtypeStruct((ROWS, WIDTH), jnp.bfloat16),
        in_specs=[pl.BlockSpec(memory_space=pltpu.VMEM)],
        out_specs=pl.BlockSpec(memory_space=pltpu.VMEM),
        compiler_params=pltpu.CompilerParams(vmem_limit_bytes=8 << 20),
        name="combine",
    )(parts)


def self_attention(query_self, key_self, value_self):
    x, zh, y = lax.axis_index("x"), lax.axis_index("zh"), lax.axis_index("y")
    group = x * NZ + zh
    kv = jnp.concatenate([key_self, value_self], axis=0)
    kvz = lax.ppermute(kv, "zh", [(0, 1), (1, 0)])
    pieces = [kv]
    groups = [group]
    for k in range(1, NX):
        pieces.append(lax.ppermute(kv, "x", [(a, a + k) for a in range(NX - k)]))
        groups.append(jnp.where(x >= k, group - NZ * k, FAR))
    pieces.append(kvz)
    groups.append(x * NZ + 1 - zh)
    for k in range(1, NX):
        pieces.append(lax.ppermute(kvz, "x", [(a, a + k) for a in range(NX - k)]))
        groups.append(jnp.where(x >= k, x * NZ + 1 - zh - NZ * k, FAR))
    q_all = lax.all_to_all(
        jnp.broadcast_to(query_self[None], (NY, ROWS, WIDTH)), "y", 0, 0, tiled=True)
    starts = jnp.stack([jnp.where(g == FAR, FAR, g * (NY * ROWS) + y * ROWS) for g in groups])
    kpos = (starts[:, None] + jnp.arange(ROWS, dtype=jnp.int32)[None, :]).reshape(1, KEYS)
    full = ((x == NX - 1) & (zh == NZ - 1)).astype(jnp.int32)
    place = jnp.stack([group * (NY * ROWS), full]).astype(jnp.int32)
    parts = partial_attention(place, kpos, q_all, pieces)
    received = lax.all_to_all(parts, "y", 0, 0, tiled=True)
    return combine(received)


def cross_attention(query_cross, neighbour_kv, neighbour_map):
    local_rows, local_width = query_cross.shape
    head_count = local_width // HD
    stretch_count = local_rows // STRETCH
    slot_count, block_len, features = neighbour_kv.shape
    group_count = features // (2 * local_width)
    stretch_first = lax.axis_index(("x", "zh", "y")) * stretch_count
    keep_stretch = stretch_first + jnp.arange(stretch_count, dtype=jnp.int32) > 0
    parted = neighbour_kv.reshape(slot_count, block_len, group_count, 2 * local_width)
    received = lax.all_to_all(parted, ("sec", "head"), split_axis=2, concat_axis=0, tiled=True)
    received = received.reshape(group_count * slot_count, block_len, 2, head_count, HD)
    chosen = received[neighbour_map]
    chosen = chosen.reshape(stretch_count, neighbour_map.shape[1] * block_len, 2, head_count, HD)
    stretch_queries = query_cross.reshape(stretch_count, STRETCH, head_count, HD)
    scores = jnp.einsum("cqhd,ckhd->chqk", stretch_queries, chosen[:, :, 0],
                        preferred_element_type=jnp.float32) * SCALE
    row_top = jnp.max(scores, axis=-1, keepdims=True)
    exp_scores = jnp.exp(scores - row_top)
    row_total = jnp.sum(exp_scores, axis=-1)
    summed = jnp.einsum("chqk,ckhd->cqhd", exp_scores.astype(jnp.bfloat16), chosen[:, :, 1],
                        preferred_element_type=jnp.float32)
    attended = summed / jnp.transpose(row_total, (0, 2, 1))[:, :, :, None]
    attended = attended.reshape(local_rows, local_width)
    keep_rows = jnp.repeat(keep_stretch, STRETCH)
    return jnp.where(keep_rows[:, None], attended, 0.0).astype(jnp.bfloat16)


def on_device(query_self, key_self, value_self, query_cross, neighbour_kv, neighbour_map):
    self_out = self_attention(query_self, key_self, value_self)
    cross_out = cross_attention(query_cross, neighbour_kv, neighbour_map)
    return (self_out, cross_out)


def solution(mesh):
    fine = Mesh(mesh.devices.reshape(2, NX, NZ, NY, 4), ("sec", "x", "zh", "y", "head"))
    rows, cols = ("x", "zh", "y"), ("sec", "head")
    return jax.shard_map(
        on_device,
        mesh=fine,
        in_specs=(
            P(rows, cols),
            P(rows, cols),
            P(rows, cols),
            P(rows, cols),
            P(("sec", "x", "zh", "y", "head"), None, None),
            P(rows, None),
        ),
        out_specs=(P(rows, cols), P(rows, cols)),
        check_vma=False,
    )
```

```python
import functools
import math

import jax
import jax.numpy as jnp
from jax import lax
from jax.experimental import pallas as pl
from jax.experimental.pallas import tpu as pltpu
from jax.sharding import Mesh
from jax.sharding import PartitionSpec as P

HD = 128
STRETCH = 64
NX, NZ, NY = 4, 2, 8
ROWS = 192
WIDTH = 256
STAT_ROWS = 16
PIECES = NX * NZ
KEYS = PIECES * ROWS
CHUNK = 256
BLOCK = 128
GROUPS = 8
GROUP_WIDTH = 512
STRETCHES = ROWS // STRETCH
LOW = -1e30
SCALE = 1.0 / math.sqrt(HD)
C2 = SCALE * math.log2(math.e)
SHARDS = 4
TILE = SHARDS * ROWS

ANY = pl.BlockSpec(memory_space=pl.ANY)
IN_SMEM = pl.BlockSpec(memory_space=pltpu.SMEM)
IN_VMEM = pl.BlockSpec(memory_space=pltpu.VMEM)


def code_stat(stat):
    row = jnp.transpose(stat)[0:STAT_ROWS // 2, :]
    hi = row.astype(jnp.bfloat16).astype(jnp.float32)
    mid = (row - hi).astype(jnp.bfloat16).astype(jnp.float32)
    low = row - hi - mid
    at = lax.broadcasted_iota(jnp.int32, row.shape, 0)
    return jnp.where(at == 0, hi, jnp.where(at == 1, mid, low))


def partial_kernel(place_ref, q_ref, *refs):
    pieces, out_ref = refs[:PIECES], refs[PIECES]
    k_scr, v_scr, s_scr, sem = refs[PIECES + 1:]
    x, zh, y = place_ref[0], place_ref[1], place_ref[2]
    i = pl.program_id(0)

    @pl.when(i == 0)
    def _():
        copies = []
        for p, kv in enumerate(pieces):
            for h in range(2):
                copies.append(pltpu.make_async_copy(
                    kv.at[pl.ds(0, ROWS), pl.ds(h * HD, HD)],
                    k_scr.at[pl.ds(p * ROWS, ROWS), pl.ds(2 * h * HD, HD)], sem.at[p, h]))
                copies.append(pltpu.make_async_copy(
                    kv.at[pl.ds(ROWS, ROWS), pl.ds(h * HD, HD)],
                    v_scr.at[pl.ds(p * ROWS, ROWS), pl.ds(2 * h * HD, HD)], sem.at[p, 2 + h]))
        for c in copies:
            c.start()
        v_scr[:, HD:2 * HD] = jnp.ones((KEYS, HD), jnp.bfloat16)
        lane0 = lax.broadcasted_iota(jnp.int32, (ROWS, HD), 1) == 0
        for p in range(PIECES):
            hidden = jnp.logical_or(x < p % NX, jnp.logical_and(zh == 0, p == NX))
            bias = jnp.where(hidden, LOW, 0.0)
            k_scr[pl.ds(p * ROWS, ROWS), HD:2 * HD] = jnp.where(lane0, bias, 0.0).astype(jnp.bfloat16)
        for c in copies:
            c.wait()

    one = jnp.where(lax.broadcasted_iota(jnp.int32, (TILE, HD), 1) == 0, 1.0, 0.0).astype(jnp.bfloat16)
    row = lax.broadcasted_iota(jnp.int32, (TILE, CHUNK), 0)
    col = lax.broadcasted_iota(jnp.int32, (TILE, CHUNK), 1)
    seen = jnp.logical_or(col >= ROWS, col - row <= i * TILE - y * ROWS)
    coded = []
    for h in range(2):
        qh = q_ref[:, :, h * HD:(h + 1) * HD].reshape(TILE, HD)
        qh = jnp.concatenate([qh, one] if h == 0 else [one, qh], axis=1)
        top = jnp.full((TILE, HD), LOW, jnp.float32)
        for c in range(KEYS // CHUNK):
            kc = k_scr[pl.ds(c * CHUNK, CHUNK), h * HD:(h + 2) * HD]
            s = lax.dot_general(qh, kc, (((1,), (1,)), ((), ())), preferred_element_type=jnp.float32)
            if c == 0:
                s = jnp.where(seen, s, LOW)
            s_scr[:, c * CHUNK:(c + 1) * CHUNK] = s
            top = jnp.maximum(top, jnp.maximum(s[:, :HD], s[:, HD:]))
        top = jnp.broadcast_to(jnp.max(top, axis=1, keepdims=True), (TILE, HD))
        off = jnp.maximum(top, -1e20) * C2
        off = jnp.concatenate([off, off], axis=1)
        acc = None
        for c in range(KEYS // CHUNK):
            p = jnp.exp2(s_scr[:, c * CHUNK:(c + 1) * CHUNK] * C2 - off).astype(jnp.bfloat16)
            d = lax.dot_general(p, v_scr[pl.ds(c * CHUNK, CHUNK), h * HD:(h + 2) * HD],
                                (((1,), (0,)), ((), ())), preferred_element_type=jnp.float32)
            acc = d if acc is None else acc + d
        main, total = (acc[:, :HD], acc[:, HD:]) if h == 0 else (acc[:, HD:], acc[:, :HD])
        total = jnp.maximum(total, 1e-30)
        out_ref[:, 0:ROWS, h * HD:(h + 1) * HD] = (main / total).astype(jnp.bfloat16).reshape(
            SHARDS, ROWS, HD)
        stat = jnp.where(top > 0.5 * LOW, top * SCALE + jnp.log(total), LOW)
        coded.append([code_stat(stat[j * ROWS:(j + 1) * ROWS]) for j in range(SHARDS)])
    for j in range(SHARDS):
        out_ref[j, ROWS:, 0:ROWS] = jnp.concatenate([coded[0][j], coded[1][j]], axis=0).astype(jnp.bfloat16)
        out_ref[j, ROWS:, ROWS:] = jnp.zeros((STAT_ROWS, WIDTH - ROWS), jnp.bfloat16)


def partial_attention(place, q_all, pieces):
    return pl.pallas_call(
        partial_kernel,
        out_shape=jax.ShapeDtypeStruct((NY, ROWS + STAT_ROWS, WIDTH), jnp.bfloat16),
        grid=(NY // SHARDS,),
        in_specs=[IN_SMEM, pl.BlockSpec((SHARDS, ROWS, WIDTH), lambda i: (i, 0, 0))] + [ANY] * PIECES,
        out_specs=pl.BlockSpec((SHARDS, ROWS + STAT_ROWS, WIDTH), lambda i: (i, 0, 0)),
        scratch_shapes=[
            pltpu.VMEM((KEYS, 3 * HD), jnp.bfloat16),
            pltpu.VMEM((KEYS, 3 * HD), jnp.bfloat16),
            pltpu.VMEM((TILE, KEYS), jnp.float32),
            pltpu.SemaphoreType.DMA((PIECES, 4)),
        ],
        cost_estimate=pl.CostEstimate(
            flops=4 * NY * ROWS * KEYS * WIDTH, bytes_accessed=4 * KEYS * WIDTH,
            transcendentals=2 * NY * ROWS * KEYS),
        compiler_params=pltpu.CompilerParams(vmem_limit_bytes=18 << 20),
        name="partial_attention",
    )(place, q_all, *pieces)


def combine_kernel(part_ref, out_ref):
    parts = [part_ref.at[j] for j in range(NY)]
    stats = []
    for h in range(2):
        rows = []
        for part in parts:
            b = part[pl.ds(ROWS, STAT_ROWS), :].astype(jnp.float32)[8 * h:8 * h + 8]
            rows.append(b[0:1] + b[1:2] + b[2:3])
        top = functools.reduce(jnp.maximum, rows)
        ws = [jnp.exp(r - top) for r in rows]
        inv = 1.0 / functools.reduce(jnp.add, ws)
        stats += [w * inv for w in ws]
    cols = jnp.transpose(jnp.concatenate(stats, axis=0))[0:ROWS]
    for h in range(2):
        acc = jnp.zeros((ROWS, HD), jnp.float32)
        for j, part in enumerate(parts):
            o = part[0:ROWS, h * HD:(h + 1) * HD].astype(jnp.float32)
            acc = acc + o * cols[:, h * NY + j:h * NY + j + 1]
        out_ref[:, h * HD:(h + 1) * HD] = acc.astype(jnp.bfloat16)


def combine(parts):
    return pl.pallas_call(
        combine_kernel,
        out_shape=jax.ShapeDtypeStruct((ROWS, WIDTH), jnp.bfloat16),
        in_specs=[IN_VMEM],
        out_specs=IN_VMEM,
        compiler_params=pltpu.CompilerParams(vmem_limit_bytes=8 << 20),
        name="combine",
    )(parts)


def split_kernel(place_ref, nkv_ref, *refs):
    outs, sem = refs[:GROUPS - 1], refs[GROUPS - 1]
    me = place_ref[3]
    copies = []
    for k in range(1, GROUPS):
        at = pl.multiple_of((me ^ k) * GROUP_WIDTH, GROUP_WIDTH)
        copies.append(pltpu.make_async_copy(
            nkv_ref.at[0, :, pl.ds(at, GROUP_WIDTH)], outs[k - 1], sem.at[k - 1]))
    for c in copies:
        c.start()
    for c in copies:
        c.wait()


def split_groups(place, neighbour_kv):
    piece = jax.ShapeDtypeStruct((BLOCK, GROUP_WIDTH), jnp.bfloat16)
    return pl.pallas_call(
        split_kernel,
        out_shape=[piece] * (GROUPS - 1),
        in_specs=[IN_SMEM, ANY],
        out_specs=[IN_VMEM] * (GROUPS - 1),
        scratch_shapes=[pltpu.SemaphoreType.DMA((GROUPS - 1,))],
        compiler_params=pltpu.CompilerParams(vmem_limit_bytes=8 << 20),
        name="split_groups",
    )(place, neighbour_kv)


def cross_kernel(place_ref, map_ref, q_ref, nkv_ref, *refs):
    pieces = refs[:GROUPS - 1]
    out_ref, scr, sem = refs[GROUPS - 1:]
    me = place_ref[3]
    at = pl.multiple_of(me * GROUP_WIDTH, GROUP_WIDTH)
    copies = [pltpu.make_async_copy(
        nkv_ref.at[0, :, pl.ds(at, GROUP_WIDTH)], scr.at[0], sem.at[0])]
    for k in range(1, GROUPS):
        copies.append(pltpu.make_async_copy(pieces[k - 1], scr.at[k], sem.at[k]))
    for c in copies:
        c.start()
    for c in copies:
        c.wait()
    for c in range(STRETCHES):
        slots = [map_ref[c, r] ^ me for r in range(2)]
        keep = place_ref[4] * STRETCHES + c > 0
        for h in range(2):
            qh = q_ref[c * STRETCH:(c + 1) * STRETCH, h * HD:(h + 1) * HD]
            s = [lax.dot_general(qh, scr[slot, :, h * HD:(h + 1) * HD], (((1,), (1,)), ((), ())),
                                 preferred_element_type=jnp.float32) for slot in slots]
            top = jnp.max(jnp.maximum(s[0], s[1]), axis=1, keepdims=True) * C2
            p = [jnp.exp2(a * C2 - top) for a in s]
            total = jnp.sum(p[0] + p[1], axis=1, keepdims=True)
            o = sum(lax.dot_general(a.astype(jnp.bfloat16), scr[slot, :, WIDTH + h * HD:WIDTH + (h + 1) * HD],
                                    (((1,), (0,)), ((), ())), preferred_element_type=jnp.float32)
                    for a, slot in zip(p, slots))
            out_ref[c * STRETCH:(c + 1) * STRETCH, h * HD:(h + 1) * HD] = jnp.where(
                keep, o / total, 0.0).astype(jnp.bfloat16)


def cross(place, neighbour_map, query_cross, neighbour_kv, pieces):
    return pl.pallas_call(
        cross_kernel,
        out_shape=jax.ShapeDtypeStruct((ROWS, WIDTH), jnp.bfloat16),
        in_specs=[IN_SMEM, IN_SMEM, IN_VMEM, ANY] + [ANY] * (GROUPS - 1),
        out_specs=IN_VMEM,
        scratch_shapes=[
            pltpu.VMEM((GROUPS, BLOCK, GROUP_WIDTH), jnp.bfloat16),
            pltpu.SemaphoreType.DMA((GROUPS,)),
        ],
        cost_estimate=pl.CostEstimate(
            flops=8 * ROWS * 2 * BLOCK * WIDTH, bytes_accessed=2 << 20, transcendentals=4 * ROWS * BLOCK),
        compiler_params=pltpu.CompilerParams(vmem_limit_bytes=8 << 20),
        name="cross_attention",
    )(place, neighbour_map, query_cross, neighbour_kv, *pieces)


def on_device(query_self, key_self, value_self, query_cross, neighbour_kv, neighbour_map):
    x, zh, y = lax.axis_index("x"), lax.axis_index("zh"), lax.axis_index("y")
    me = lax.axis_index(("sec", "head"))
    place = jnp.stack([x, zh, y, me, lax.axis_index(("x", "zh", "y"))]).astype(jnp.int32)

    kv = jnp.concatenate([key_self, value_self], axis=0)
    kvz = lax.ppermute(kv, "zh", [(0, 1), (1, 0)])
    pieces = [kv]
    for k in range(1, NX):
        pieces.append(lax.ppermute(kv, "x", [(a, a + k) for a in range(NX - k)]))
    pieces.append(kvz)
    for k in range(1, NX):
        pieces.append(lax.ppermute(kvz, "x", [(a, a + k) for a in range(NX - k)]))
    q_all = lax.all_to_all(
        jnp.broadcast_to(query_self[None], (NY, ROWS, WIDTH)), "y", 0, 0, tiled=True)

    outgoing = split_groups(place, neighbour_kv)
    arrived = [lax.ppermute(outgoing[k - 1], ("sec", "head"), [(a, a ^ k) for a in range(GROUPS)])
               for k in range(1, GROUPS)]

    parts = partial_attention(place, q_all, pieces)
    received = lax.all_to_all(parts, "y", 0, 0, tiled=True)
    self_out = combine(received)
    cross_out = cross(place, neighbour_map, query_cross, neighbour_kv, arrived)
    return (self_out, cross_out)


def solution(mesh):
    fine = Mesh(mesh.devices.reshape(2, NX, NZ, NY, 4), ("sec", "x", "zh", "y", "head"))
    rows, cols = ("x", "zh", "y"), ("sec", "head")
    return jax.shard_map(
        on_device,
        mesh=fine,
        in_specs=(
            P(rows, cols),
            P(rows, cols),
            P(rows, cols),
            P(rows, cols),
            P(("sec", "x", "zh", "y", "head"), None, None),
            P(rows, None),
        ),
        out_specs=(P(rows, cols), P(rows, cols)),
        check_vma=False,
    )
```

```python
import functools
import math

import jax
import jax.numpy as jnp
from jax import lax
from jax.experimental import pallas as pl
from jax.experimental.pallas import tpu as pltpu
from jax.sharding import Mesh
from jax.sharding import PartitionSpec as P

HD = 128
STRETCH = 64
NX, NZ, NY = 4, 2, 8
ROWS = 192
WIDTH = 256
STAT_ROWS = 16
PIECES = NX * NZ
KEYS = PIECES * ROWS
CHUNK = 256
BLOCK = 128
GROUPS = 8
HEADS = 4
GROUP_WIDTH = 512
STRETCHES = ROWS // STRETCH
LOW = -1e30
SCALE = 1.0 / math.sqrt(HD)
C2 = SCALE * math.log2(math.e)
SHARDS = 4
TILE = SHARDS * ROWS

ANY = pl.BlockSpec(memory_space=pl.ANY)
IN_SMEM = pl.BlockSpec(memory_space=pltpu.SMEM)
IN_VMEM = pl.BlockSpec(memory_space=pltpu.VMEM)


def code_stat(stat):
    row = jnp.transpose(stat)[0:STAT_ROWS // 2, :]
    hi = row.astype(jnp.bfloat16).astype(jnp.float32)
    mid = (row - hi).astype(jnp.bfloat16).astype(jnp.float32)
    low = row - hi - mid
    at = lax.broadcasted_iota(jnp.int32, row.shape, 0)
    return jnp.where(at == 0, hi, jnp.where(at == 1, mid, low))


def partial_kernel(place_ref, q_ref, *refs):
    pieces, out_ref = refs[:PIECES], refs[PIECES]
    k_scr, v_scr, s_scr, sem = refs[PIECES + 1:]
    x, zh, y = place_ref[0], place_ref[1], place_ref[2]
    i = pl.program_id(0)

    @pl.when(i == 0)
    def _():
        copies = []
        for p, kv in enumerate(pieces):
            for h in range(2):
                copies.append(pltpu.make_async_copy(
                    kv.at[pl.ds(0, ROWS), pl.ds(h * HD, HD)],
                    k_scr.at[pl.ds(p * ROWS, ROWS), pl.ds(2 * h * HD, HD)], sem.at[p, h]))
                copies.append(pltpu.make_async_copy(
                    kv.at[pl.ds(ROWS, ROWS), pl.ds(h * HD, HD)],
                    v_scr.at[pl.ds(p * ROWS, ROWS), pl.ds(2 * h * HD, HD)], sem.at[p, 2 + h]))
        for c in copies:
            c.start()
        v_scr[:, HD:2 * HD] = jnp.ones((KEYS, HD), jnp.bfloat16)
        lane0 = lax.broadcasted_iota(jnp.int32, (ROWS, HD), 1) == 0
        for p in range(PIECES):
            hidden = jnp.logical_or(x < p % NX, jnp.logical_and(zh == 0, p == NX))
            bias = jnp.where(hidden, LOW, 0.0)
            k_scr[pl.ds(p * ROWS, ROWS), HD:2 * HD] = jnp.where(lane0, bias, 0.0).astype(jnp.bfloat16)
        for c in copies:
            c.wait()

    one = jnp.where(lax.broadcasted_iota(jnp.int32, (TILE, HD), 1) == 0, 1.0, 0.0).astype(jnp.bfloat16)
    row = lax.broadcasted_iota(jnp.int32, (TILE, CHUNK), 0)
    col = lax.broadcasted_iota(jnp.int32, (TILE, CHUNK), 1)
    seen = jnp.logical_or(col >= ROWS, col - row <= i * TILE - y * ROWS)
    coded = []
    for h in range(2):
        qh = q_ref[:, :, h * HD:(h + 1) * HD].reshape(TILE, HD)
        qh = jnp.concatenate([qh, one] if h == 0 else [one, qh], axis=1)
        top = jnp.full((TILE, HD), LOW, jnp.float32)
        for c in range(KEYS // CHUNK):
            kc = k_scr[pl.ds(c * CHUNK, CHUNK), h * HD:(h + 2) * HD]
            s = lax.dot_general(qh, kc, (((1,), (1,)), ((), ())), preferred_element_type=jnp.float32)
            if c == 0:
                s = jnp.where(seen, s, LOW)
            s_scr[:, c * CHUNK:(c + 1) * CHUNK] = s
            top = jnp.maximum(top, jnp.maximum(s[:, :HD], s[:, HD:]))
        top = jnp.broadcast_to(jnp.max(top, axis=1, keepdims=True), (TILE, HD))
        off = jnp.maximum(top, -1e20) * C2
        off = jnp.concatenate([off, off], axis=1)
        acc = None
        for c in range(KEYS // CHUNK):
            p = jnp.exp2(s_scr[:, c * CHUNK:(c + 1) * CHUNK] * C2 - off).astype(jnp.bfloat16)
            d = lax.dot_general(p, v_scr[pl.ds(c * CHUNK, CHUNK), h * HD:(h + 2) * HD],
                                (((1,), (0,)), ((), ())), preferred_element_type=jnp.float32)
            acc = d if acc is None else acc + d
        main, total = (acc[:, :HD], acc[:, HD:]) if h == 0 else (acc[:, HD:], acc[:, :HD])
        total = jnp.maximum(total, 1e-30)
        out_ref[:, 0:ROWS, h * HD:(h + 1) * HD] = (main / total).astype(jnp.bfloat16).reshape(
            SHARDS, ROWS, HD)
        stat = jnp.where(top > 0.5 * LOW, top * SCALE + jnp.log(total), LOW)
        coded.append([code_stat(stat[j * ROWS:(j + 1) * ROWS]) for j in range(SHARDS)])
    for j in range(SHARDS):
        out_ref[j, ROWS:, 0:ROWS] = jnp.concatenate([coded[0][j], coded[1][j]], axis=0).astype(jnp.bfloat16)
        out_ref[j, ROWS:, ROWS:] = jnp.zeros((STAT_ROWS, WIDTH - ROWS), jnp.bfloat16)


def partial_attention(place, q_all, pieces):
    return pl.pallas_call(
        partial_kernel,
        out_shape=jax.ShapeDtypeStruct((NY, ROWS + STAT_ROWS, WIDTH), jnp.bfloat16),
        grid=(NY // SHARDS,),
        in_specs=[IN_SMEM, pl.BlockSpec((SHARDS, ROWS, WIDTH), lambda i: (i, 0, 0))] + [ANY] * PIECES,
        out_specs=pl.BlockSpec((SHARDS, ROWS + STAT_ROWS, WIDTH), lambda i: (i, 0, 0)),
        scratch_shapes=[
            pltpu.VMEM((KEYS, 3 * HD), jnp.bfloat16),
            pltpu.VMEM((KEYS, 3 * HD), jnp.bfloat16),
            pltpu.VMEM((TILE, KEYS), jnp.float32),
            pltpu.SemaphoreType.DMA((PIECES, 4)),
        ],
        cost_estimate=pl.CostEstimate(
            flops=4 * NY * ROWS * KEYS * WIDTH, bytes_accessed=4 * KEYS * WIDTH,
            transcendentals=2 * NY * ROWS * KEYS),
        compiler_params=pltpu.CompilerParams(vmem_limit_bytes=18 << 20),
        name="partial_attention",
    )(place, q_all, *pieces)


def combine_kernel(part_ref, out_ref):
    parts = [part_ref.at[j] for j in range(NY)]
    stats = []
    for h in range(2):
        rows = []
        for part in parts:
            b = part[pl.ds(ROWS, STAT_ROWS), :].astype(jnp.float32)[8 * h:8 * h + 8]
            rows.append(b[0:1] + b[1:2] + b[2:3])
        top = functools.reduce(jnp.maximum, rows)
        ws = [jnp.exp(r - top) for r in rows]
        inv = 1.0 / functools.reduce(jnp.add, ws)
        stats += [w * inv for w in ws]
    cols = jnp.transpose(jnp.concatenate(stats, axis=0))[0:ROWS]
    for h in range(2):
        acc = jnp.zeros((ROWS, HD), jnp.float32)
        for j, part in enumerate(parts):
            o = part[0:ROWS, h * HD:(h + 1) * HD].astype(jnp.float32)
            acc = acc + o * cols[:, h * NY + j:h * NY + j + 1]
        out_ref[:, h * HD:(h + 1) * HD] = acc.astype(jnp.bfloat16)


def combine(parts):
    return pl.pallas_call(
        combine_kernel,
        out_shape=jax.ShapeDtypeStruct((ROWS, WIDTH), jnp.bfloat16),
        in_specs=[IN_VMEM],
        out_specs=IN_VMEM,
        compiler_params=pltpu.CompilerParams(vmem_limit_bytes=8 << 20),
        name="combine",
    )(parts)


def split_kernel(place_ref, nkv_ref, twin_ref, *refs):
    outs, sem = refs[:HEADS - 1], refs[HEADS - 1]
    me = place_ref[3]
    copies = []
    for k in range(1, HEADS):
        at = pl.multiple_of((me ^ k) * GROUP_WIDTH, GROUP_WIDTH)
        near = pl.multiple_of(((me ^ k) & (HEADS - 1)) * GROUP_WIDTH, GROUP_WIDTH)
        copies.append(pltpu.make_async_copy(
            nkv_ref.at[0, :, pl.ds(at, GROUP_WIDTH)], outs[k - 1].at[0], sem.at[k - 1, 0]))
        copies.append(pltpu.make_async_copy(
            twin_ref.at[:, pl.ds(near, GROUP_WIDTH)], outs[k - 1].at[1], sem.at[k - 1, 1]))
    for c in copies:
        c.start()
    for c in copies:
        c.wait()


def split_groups(place, neighbour_kv, twin):
    piece = jax.ShapeDtypeStruct((2, BLOCK, GROUP_WIDTH), jnp.bfloat16)
    return pl.pallas_call(
        split_kernel,
        out_shape=[piece] * (HEADS - 1),
        in_specs=[IN_SMEM, ANY, ANY],
        out_specs=[IN_VMEM] * (HEADS - 1),
        scratch_shapes=[pltpu.SemaphoreType.DMA((HEADS - 1, 2))],
        compiler_params=pltpu.CompilerParams(vmem_limit_bytes=8 << 20),
        name="split_groups",
    )(place, neighbour_kv, twin)


def cross_kernel(place_ref, map_ref, q_ref, nkv_ref, twin_ref, *refs):
    pieces = refs[:HEADS - 1]
    out_ref, scr, sem = refs[HEADS - 1:]
    me = place_ref[3]
    at = pl.multiple_of(me * GROUP_WIDTH, GROUP_WIDTH)
    near = pl.multiple_of((me & (HEADS - 1)) * GROUP_WIDTH, GROUP_WIDTH)
    copies = [
        pltpu.make_async_copy(nkv_ref.at[0, :, pl.ds(at, GROUP_WIDTH)], scr.at[0], sem.at[0]),
        pltpu.make_async_copy(twin_ref.at[:, pl.ds(near, GROUP_WIDTH)], scr.at[1], sem.at[1]),
    ]
    for k in range(1, HEADS):
        copies.append(pltpu.make_async_copy(pieces[k - 1], scr.at[pl.ds(2 * k, 2)], sem.at[2 * k]))
    for c in copies:
        c.start()
    for c in copies:
        c.wait()
    for c in range(STRETCHES):
        flips = [map_ref[c, r] ^ me for r in range(2)]
        slots = [(f & (HEADS - 1)) * 2 + ((f >> 2) & 1) for f in flips]
        keep = place_ref[4] * STRETCHES + c > 0
        for h in range(2):
            qh = q_ref[c * STRETCH:(c + 1) * STRETCH, h * HD:(h + 1) * HD]
            s = [lax.dot_general(qh, scr[slot, :, h * HD:(h + 1) * HD], (((1,), (1,)), ((), ())),
                                 preferred_element_type=jnp.float32) for slot in slots]
            top = jnp.max(jnp.maximum(s[0], s[1]), axis=1, keepdims=True) * C2
            p = [jnp.exp2(a * C2 - top) for a in s]
            total = jnp.sum(p[0] + p[1], axis=1, keepdims=True)
            o = sum(lax.dot_general(a.astype(jnp.bfloat16), scr[slot, :, WIDTH + h * HD:WIDTH + (h + 1) * HD],
                                    (((1,), (0,)), ((), ())), preferred_element_type=jnp.float32)
                    for a, slot in zip(p, slots))
            out_ref[c * STRETCH:(c + 1) * STRETCH, h * HD:(h + 1) * HD] = jnp.where(
                keep, o / total, 0.0).astype(jnp.bfloat16)


def cross(place, neighbour_map, query_cross, neighbour_kv, twin, pieces):
    return pl.pallas_call(
        cross_kernel,
        out_shape=jax.ShapeDtypeStruct((ROWS, WIDTH), jnp.bfloat16),
        in_specs=[IN_SMEM, IN_SMEM, IN_VMEM, ANY, ANY] + [ANY] * (HEADS - 1),
        out_specs=IN_VMEM,
        scratch_shapes=[
            pltpu.VMEM((GROUPS, BLOCK, GROUP_WIDTH), jnp.bfloat16),
            pltpu.SemaphoreType.DMA((GROUPS,)),
        ],
        cost_estimate=pl.CostEstimate(
            flops=8 * ROWS * 2 * BLOCK * WIDTH, bytes_accessed=2 << 20, transcendentals=4 * ROWS * BLOCK),
        compiler_params=pltpu.CompilerParams(vmem_limit_bytes=8 << 20),
        name="cross_attention",
    )(place, neighbour_map, query_cross, neighbour_kv, twin, *pieces)


def on_device(query_self, key_self, value_self, query_cross, neighbour_kv, neighbour_map):
    x, zh, y = lax.axis_index("x"), lax.axis_index("zh"), lax.axis_index("y")
    me = lax.axis_index(("sec", "head"))
    place = jnp.stack([x, zh, y, me, lax.axis_index(("x", "zh", "y"))]).astype(jnp.int32)

    kv = jnp.concatenate([key_self, value_self], axis=0)
    kvz = lax.ppermute(kv, "zh", [(0, 1), (1, 0)])
    pieces = [kv]
    for k in range(1, NX):
        pieces.append(lax.ppermute(kv, "x", [(a, a + k) for a in range(NX - k)]))
    pieces.append(kvz)
    for k in range(1, NX):
        pieces.append(lax.ppermute(kvz, "x", [(a, a + k) for a in range(NX - k)]))
    q_all = lax.all_to_all(
        jnp.broadcast_to(query_self[None], (NY, ROWS, WIDTH)), "y", 0, 0, tiled=True)

    half = HEADS * GROUP_WIDTH
    mine = lax.dynamic_slice(
        neighbour_kv[0], (0, (1 - lax.axis_index("sec")) * half), (BLOCK, half))
    twin = lax.ppermute(mine, "sec", [(0, 1), (1, 0)])
    outgoing = split_groups(place, neighbour_kv, twin)
    arrived = [lax.ppermute(outgoing[k - 1], "head", [(a, a ^ k) for a in range(HEADS)])
               for k in range(1, HEADS)]

    parts = partial_attention(place, q_all, pieces)
    cross_out = cross(place, neighbour_map, query_cross, neighbour_kv, twin, arrived)
    parts, cross_out = lax.optimization_barrier((parts, cross_out))
    received = lax.all_to_all(parts, "y", 0, 0, tiled=True)
    self_out = combine(received)
    return (self_out, cross_out)


def solution(mesh):
    fine = Mesh(mesh.devices.reshape(2, NX, NZ, NY, 4), ("sec", "x", "zh", "y", "head"))
    rows, cols = ("x", "zh", "y"), ("sec", "head")
    return jax.shard_map(
        on_device,
        mesh=fine,
        in_specs=(
            P(rows, cols),
            P(rows, cols),
            P(rows, cols),
            P(rows, cols),
            P(("sec", "x", "zh", "y", "head"), None, None),
            P(rows, None),
        ),
        out_specs=(P(rows, cols), P(rows, cols)),
        check_vma=False,
    )
```

```python
import functools
import math

import jax
import jax.numpy as jnp
from jax import lax
from jax.experimental import pallas as pl
from jax.experimental.pallas import tpu as pltpu
from jax.sharding import Mesh
from jax.sharding import PartitionSpec as P

HD = 128
STRETCH = 64
NX, NZ, NY = 4, 2, 8
ROWS = 192
WIDTH = 256
STAT_ROWS = 16
PIECES = NX * NZ
KEYS = PIECES * ROWS
CHUNK = 256
BLOCK = 128
GROUPS = 8
HEADS = 4
GROUP_WIDTH = 512
STRETCHES = ROWS // STRETCH
LOW = -1e30
SCALE = 1.0 / math.sqrt(HD)
C2 = SCALE * math.log2(math.e)
SHARDS = 4
TILE = SHARDS * ROWS

ANY = pl.BlockSpec(memory_space=pl.ANY)
IN_SMEM = pl.BlockSpec(memory_space=pltpu.SMEM)
IN_VMEM = pl.BlockSpec(memory_space=pltpu.VMEM)


def code_stat(stat):
    row = jnp.transpose(stat)[0:STAT_ROWS // 2, :]
    hi = row.astype(jnp.bfloat16).astype(jnp.float32)
    mid = (row - hi).astype(jnp.bfloat16).astype(jnp.float32)
    low = row - hi - mid
    at = lax.broadcasted_iota(jnp.int32, row.shape, 0)
    return jnp.where(at == 0, hi, jnp.where(at == 1, mid, low))


def partial_kernel(place_ref, q_ref, *refs):
    pieces, out_ref = refs[:NX], refs[NX]
    k_scr, v_scr, s_scr, sem = refs[NX + 1:]
    x, zh, y = place_ref[0], place_ref[1], place_ref[2]
    i = pl.program_id(0)

    @pl.when(i == 0)
    def _():
        copies = []
        for p in range(PIECES):
            kv, at = pieces[p % NX], p // NX * 2 * ROWS
            for h in range(2):
                copies.append(pltpu.make_async_copy(
                    kv.at[pl.ds(at, ROWS), pl.ds(h * HD, HD)],
                    k_scr.at[pl.ds(p * ROWS, ROWS), pl.ds(2 * h * HD, HD)], sem.at[p, h]))
                copies.append(pltpu.make_async_copy(
                    kv.at[pl.ds(at + ROWS, ROWS), pl.ds(h * HD, HD)],
                    v_scr.at[pl.ds(p * ROWS, ROWS), pl.ds(2 * h * HD, HD)], sem.at[p, 2 + h]))
        for c in copies:
            c.start()
        v_scr[:, HD:2 * HD] = jnp.ones((KEYS, HD), jnp.bfloat16)
        lane0 = lax.broadcasted_iota(jnp.int32, (ROWS, HD), 1) == 0
        for p in range(PIECES):
            hidden = jnp.logical_or(x < p % NX, jnp.logical_and(zh == 0, p == NX))
            bias = jnp.where(hidden, LOW, 0.0)
            k_scr[pl.ds(p * ROWS, ROWS), HD:2 * HD] = jnp.where(lane0, bias, 0.0).astype(jnp.bfloat16)
        for c in copies:
            c.wait()

    one = jnp.where(lax.broadcasted_iota(jnp.int32, (TILE, HD), 1) == 0, 1.0, 0.0).astype(jnp.bfloat16)
    row = lax.broadcasted_iota(jnp.int32, (TILE, CHUNK), 0)
    col = lax.broadcasted_iota(jnp.int32, (TILE, CHUNK), 1)
    seen = jnp.logical_or(col >= ROWS, col - row <= i * TILE - y * ROWS)
    coded = []
    for h in range(2):
        qh = q_ref[:, :, h * HD:(h + 1) * HD].reshape(TILE, HD)
        qh = jnp.concatenate([qh, one] if h == 0 else [one, qh], axis=1)
        top = jnp.full((TILE, HD), LOW, jnp.float32)
        for c in range(KEYS // CHUNK):
            kc = k_scr[pl.ds(c * CHUNK, CHUNK), h * HD:(h + 2) * HD]
            s = lax.dot_general(qh, kc, (((1,), (1,)), ((), ())), preferred_element_type=jnp.float32)
            if c == 0:
                s = jnp.where(seen, s, LOW)
            s_scr[:, c * CHUNK:(c + 1) * CHUNK] = s
            top = jnp.maximum(top, jnp.maximum(s[:, :HD], s[:, HD:]))
        top = jnp.broadcast_to(jnp.max(top, axis=1, keepdims=True), (TILE, HD))
        off = jnp.maximum(top, -1e20) * C2
        off = jnp.concatenate([off, off], axis=1)
        acc = None
        for c in range(KEYS // CHUNK):
            p = jnp.exp2(s_scr[:, c * CHUNK:(c + 1) * CHUNK] * C2 - off).astype(jnp.bfloat16)
            d = lax.dot_general(p, v_scr[pl.ds(c * CHUNK, CHUNK), h * HD:(h + 2) * HD],
                                (((1,), (0,)), ((), ())), preferred_element_type=jnp.float32)
            acc = d if acc is None else acc + d
        main, total = (acc[:, :HD], acc[:, HD:]) if h == 0 else (acc[:, HD:], acc[:, :HD])
        total = jnp.maximum(total, 1e-30)
        out_ref[:, 0:ROWS, h * HD:(h + 1) * HD] = (main / total).astype(jnp.bfloat16).reshape(
            SHARDS, ROWS, HD)
        stat = jnp.where(top > 0.5 * LOW, top * SCALE + jnp.log(total), LOW)
        coded.append([code_stat(stat[j * ROWS:(j + 1) * ROWS]) for j in range(SHARDS)])
    for j in range(SHARDS):
        out_ref[j, ROWS:, 0:ROWS] = jnp.concatenate([coded[0][j], coded[1][j]], axis=0).astype(jnp.bfloat16)
        out_ref[j, ROWS:, ROWS:] = jnp.zeros((STAT_ROWS, WIDTH - ROWS), jnp.bfloat16)


def partial_attention(place, q_all, pieces):
    return pl.pallas_call(
        partial_kernel,
        out_shape=jax.ShapeDtypeStruct((NY, ROWS + STAT_ROWS, WIDTH), jnp.bfloat16),
        grid=(NY // SHARDS,),
        in_specs=[IN_SMEM, pl.BlockSpec((SHARDS, ROWS, WIDTH), lambda i: (i, 0, 0))] + [ANY] * NX,
        out_specs=pl.BlockSpec((SHARDS, ROWS + STAT_ROWS, WIDTH), lambda i: (i, 0, 0)),
        scratch_shapes=[
            pltpu.VMEM((KEYS, 3 * HD), jnp.bfloat16),
            pltpu.VMEM((KEYS, 3 * HD), jnp.bfloat16),
            pltpu.VMEM((TILE, KEYS), jnp.float32),
            pltpu.SemaphoreType.DMA((PIECES, 4)),
        ],
        cost_estimate=pl.CostEstimate(
            flops=4 * NY * ROWS * KEYS * WIDTH, bytes_accessed=4 * KEYS * WIDTH,
            transcendentals=2 * NY * ROWS * KEYS),
        compiler_params=pltpu.CompilerParams(vmem_limit_bytes=18 << 20),
        name="partial_attention",
    )(place, q_all, *pieces)


def combine_kernel(part_ref, out_ref):
    parts = [part_ref.at[j] for j in range(NY)]
    stats = []
    for h in range(2):
        rows = []
        for part in parts:
            b = part[pl.ds(ROWS, STAT_ROWS), :].astype(jnp.float32)[8 * h:8 * h + 8]
            rows.append(b[0:1] + b[1:2] + b[2:3])
        top = functools.reduce(jnp.maximum, rows)
        ws = [jnp.exp(r - top) for r in rows]
        inv = 1.0 / functools.reduce(jnp.add, ws)
        stats += [w * inv for w in ws]
    cols = jnp.transpose(jnp.concatenate(stats, axis=0))[0:ROWS]
    for h in range(2):
        acc = jnp.zeros((ROWS, HD), jnp.float32)
        for j, part in enumerate(parts):
            o = part[0:ROWS, h * HD:(h + 1) * HD].astype(jnp.float32)
            acc = acc + o * cols[:, h * NY + j:h * NY + j + 1]
        out_ref[:, h * HD:(h + 1) * HD] = acc.astype(jnp.bfloat16)


def combine(parts):
    return pl.pallas_call(
        combine_kernel,
        out_shape=jax.ShapeDtypeStruct((ROWS, WIDTH), jnp.bfloat16),
        in_specs=[IN_VMEM],
        out_specs=IN_VMEM,
        compiler_params=pltpu.CompilerParams(vmem_limit_bytes=8 << 20),
        name="combine",
    )(parts)


def split_kernel(place_ref, nkv_ref, twin_ref, *refs):
    outs, sem = refs[:HEADS - 1], refs[HEADS - 1]
    me = place_ref[3]
    copies = []
    for k in range(1, HEADS):
        at = pl.multiple_of((me ^ k) * GROUP_WIDTH, GROUP_WIDTH)
        near = pl.multiple_of(((me ^ k) & (HEADS - 1)) * GROUP_WIDTH, GROUP_WIDTH)
        copies.append(pltpu.make_async_copy(
            nkv_ref.at[0, :, pl.ds(at, GROUP_WIDTH)], outs[k - 1].at[0], sem.at[k - 1, 0]))
        copies.append(pltpu.make_async_copy(
            twin_ref.at[:, pl.ds(near, GROUP_WIDTH)], outs[k - 1].at[1], sem.at[k - 1, 1]))
    for c in copies:
        c.start()
    for c in copies:
        c.wait()


def split_groups(place, neighbour_kv, twin):
    piece = jax.ShapeDtypeStruct((2, BLOCK, GROUP_WIDTH), jnp.bfloat16)
    return pl.pallas_call(
        split_kernel,
        out_shape=[piece] * (HEADS - 1),
        in_specs=[IN_SMEM, ANY, ANY],
        out_specs=[IN_VMEM] * (HEADS - 1),
        scratch_shapes=[pltpu.SemaphoreType.DMA((HEADS - 1, 2))],
        compiler_params=pltpu.CompilerParams(vmem_limit_bytes=8 << 20),
        name="split_groups",
    )(place, neighbour_kv, twin)


def cross_kernel(place_ref, map_ref, q_ref, nkv_ref, twin_ref, *refs):
    pieces = refs[:HEADS - 1]
    out_ref, scr, sem = refs[HEADS - 1:]
    me = place_ref[3]
    at = pl.multiple_of(me * GROUP_WIDTH, GROUP_WIDTH)
    near = pl.multiple_of((me & (HEADS - 1)) * GROUP_WIDTH, GROUP_WIDTH)
    copies = [
        pltpu.make_async_copy(nkv_ref.at[0, :, pl.ds(at, GROUP_WIDTH)], scr.at[0], sem.at[0]),
        pltpu.make_async_copy(twin_ref.at[:, pl.ds(near, GROUP_WIDTH)], scr.at[1], sem.at[1]),
    ]
    for k in range(1, HEADS):
        copies.append(pltpu.make_async_copy(pieces[k - 1], scr.at[pl.ds(2 * k, 2)], sem.at[2 * k]))
    for c in copies:
        c.start()
    for c in copies:
        c.wait()
    for c in range(STRETCHES):
        flips = [map_ref[c, r] ^ me for r in range(2)]
        slots = [(f & (HEADS - 1)) * 2 + ((f >> 2) & 1) for f in flips]
        keep = place_ref[4] * STRETCHES + c > 0
        for h in range(2):
            qh = q_ref[c * STRETCH:(c + 1) * STRETCH, h * HD:(h + 1) * HD]
            s = [lax.dot_general(qh, scr[slot, :, h * HD:(h + 1) * HD], (((1,), (1,)), ((), ())),
                                 preferred_element_type=jnp.float32) for slot in slots]
            top = jnp.max(jnp.maximum(s[0], s[1]), axis=1, keepdims=True) * C2
            p = [jnp.exp2(a * C2 - top) for a in s]
            total = jnp.sum(p[0] + p[1], axis=1, keepdims=True)
            o = sum(lax.dot_general(a.astype(jnp.bfloat16), scr[slot, :, WIDTH + h * HD:WIDTH + (h + 1) * HD],
                                    (((1,), (0,)), ((), ())), preferred_element_type=jnp.float32)
                    for a, slot in zip(p, slots))
            out_ref[c * STRETCH:(c + 1) * STRETCH, h * HD:(h + 1) * HD] = jnp.where(
                keep, o / total, 0.0).astype(jnp.bfloat16)


def cross(place, neighbour_map, query_cross, neighbour_kv, twin, pieces):
    return pl.pallas_call(
        cross_kernel,
        out_shape=jax.ShapeDtypeStruct((ROWS, WIDTH), jnp.bfloat16),
        in_specs=[IN_SMEM, IN_SMEM, IN_VMEM, ANY, ANY] + [ANY] * (HEADS - 1),
        out_specs=IN_VMEM,
        scratch_shapes=[
            pltpu.VMEM((GROUPS, BLOCK, GROUP_WIDTH), jnp.bfloat16),
            pltpu.SemaphoreType.DMA((GROUPS,)),
        ],
        cost_estimate=pl.CostEstimate(
            flops=8 * ROWS * 2 * BLOCK * WIDTH, bytes_accessed=2 << 20, transcendentals=4 * ROWS * BLOCK),
        compiler_params=pltpu.CompilerParams(vmem_limit_bytes=8 << 20),
        name="cross_attention",
    )(place, neighbour_map, query_cross, neighbour_kv, twin, *pieces)


def on_device(query_self, key_self, value_self, query_cross, neighbour_kv, neighbour_map):
    x, zh, y = lax.axis_index("x"), lax.axis_index("zh"), lax.axis_index("y")
    me = lax.axis_index(("sec", "head"))
    place = jnp.stack([x, zh, y, me, lax.axis_index(("x", "zh", "y"))]).astype(jnp.int32)

    kv = jnp.concatenate([key_self, value_self], axis=0)
    kvz = lax.ppermute(kv, "zh", [(0, 1), (1, 0)])
    both = jnp.concatenate([kv, kvz], axis=0)
    pieces = [both]
    for k in range(1, NX):
        pieces.append(lax.ppermute(both, "x", [(a, a + k) for a in range(NX - k)]))
    q_all = lax.all_to_all(
        jnp.broadcast_to(query_self[None], (NY, ROWS, WIDTH)), "y", 0, 0, tiled=True)

    half = HEADS * GROUP_WIDTH
    mine = lax.dynamic_slice(
        neighbour_kv[0], (0, (1 - lax.axis_index("sec")) * half), (BLOCK, half))
    twin = lax.ppermute(mine, "sec", [(0, 1), (1, 0)])
    outgoing = split_groups(place, neighbour_kv, twin)
    arrived = [lax.ppermute(outgoing[k - 1], "head", [(a, a ^ k) for a in range(HEADS)])
               for k in range(1, HEADS)]

    parts = partial_attention(place, q_all, pieces)
    cross_out = cross(place, neighbour_map, query_cross, neighbour_kv, twin, arrived)
    received = lax.all_to_all(parts, "y", 0, 0, tiled=True)
    self_out = combine(received)
    return (self_out, cross_out)


def solution(mesh):
    fine = Mesh(mesh.devices.reshape(2, NX, NZ, NY, 4), ("sec", "x", "zh", "y", "head"))
    rows, cols = ("x", "zh", "y"), ("sec", "head")
    return jax.shard_map(
        on_device,
        mesh=fine,
        in_specs=(
            P(rows, cols),
            P(rows, cols),
            P(rows, cols),
            P(rows, cols),
            P(("sec", "x", "zh", "y", "head"), None, None),
            P(rows, None),
        ),
        out_specs=(P(rows, cols), P(rows, cols)),
        check_vma=False,
    )
```

```python
import functools
import math

import jax
import jax.numpy as jnp
from jax import lax
from jax.experimental import pallas as pl
from jax.experimental.pallas import tpu as pltpu
from jax.sharding import Mesh
from jax.sharding import PartitionSpec as P

HD = 128
STRETCH = 64
NX, NZ, NY = 4, 2, 8
ROWS = 192
WIDTH = 256
STAT_ROWS = 16
PIECES = NX * NZ
KEYS = PIECES * ROWS
CHUNK = 256
BLOCK = 128
GROUPS = 8
HEADS = 4
GROUP_WIDTH = 512
STRETCHES = ROWS // STRETCH
LOW = -1e30
SCALE = 1.0 / math.sqrt(HD)
C2 = SCALE * math.log2(math.e)
SHARDS = 4
TILE = SHARDS * ROWS

ANY = pl.BlockSpec(memory_space=pl.ANY)
IN_SMEM = pl.BlockSpec(memory_space=pltpu.SMEM)
IN_VMEM = pl.BlockSpec(memory_space=pltpu.VMEM)


def code_stat(stat):
    row = jnp.transpose(stat)[0:STAT_ROWS // 2, :]
    hi = row.astype(jnp.bfloat16).astype(jnp.float32)
    mid = (row - hi).astype(jnp.bfloat16).astype(jnp.float32)
    low = row - hi - mid
    at = lax.broadcasted_iota(jnp.int32, row.shape, 0)
    return jnp.where(at == 0, hi, jnp.where(at == 1, mid, low))


def partial_kernel(place_ref, q_ref, *refs):
    pieces, out_ref = refs[:PIECES], refs[PIECES]
    k_scr, v_scr, s_scr, sem = refs[PIECES + 1:]
    x, zh, y = place_ref[0], place_ref[1], place_ref[2]
    i = pl.program_id(0)

    @pl.when(i == 0)
    def _():
        copies = []
        for p in range(PIECES):
            kv, at = pieces[p], 0
            for h in range(2):
                copies.append(pltpu.make_async_copy(
                    kv.at[pl.ds(at, ROWS), pl.ds(h * HD, HD)],
                    k_scr.at[pl.ds(p * ROWS, ROWS), pl.ds(2 * h * HD, HD)], sem.at[p, h]))
                copies.append(pltpu.make_async_copy(
                    kv.at[pl.ds(at + ROWS, ROWS), pl.ds(h * HD, HD)],
                    v_scr.at[pl.ds(p * ROWS, ROWS), pl.ds(2 * h * HD, HD)], sem.at[p, 2 + h]))
        for c in copies:
            c.start()
        v_scr[:, HD:2 * HD] = jnp.ones((KEYS, HD), jnp.bfloat16)
        lane0 = lax.broadcasted_iota(jnp.int32, (ROWS, HD), 1) == 0
        for p in range(PIECES):
            hidden = jnp.logical_or(x < p % NX, jnp.logical_and(zh == 0, p == NX))
            bias = jnp.where(hidden, LOW, 0.0)
            k_scr[pl.ds(p * ROWS, ROWS), HD:2 * HD] = jnp.where(lane0, bias, 0.0).astype(jnp.bfloat16)
        for c in copies:
            c.wait()

    one = jnp.where(lax.broadcasted_iota(jnp.int32, (TILE, HD), 1) == 0, 1.0, 0.0).astype(jnp.bfloat16)
    row = lax.broadcasted_iota(jnp.int32, (TILE, CHUNK), 0)
    col = lax.broadcasted_iota(jnp.int32, (TILE, CHUNK), 1)
    seen = jnp.logical_or(col >= ROWS, col - row <= i * TILE - y * ROWS)
    coded = []
    for h in range(2):
        qh = q_ref[:, :, h * HD:(h + 1) * HD].reshape(TILE, HD)
        qh = jnp.concatenate([qh, one] if h == 0 else [one, qh], axis=1)
        top = jnp.full((TILE, HD), LOW, jnp.float32)
        for c in range(KEYS // CHUNK):
            kc = k_scr[pl.ds(c * CHUNK, CHUNK), h * HD:(h + 2) * HD]
            s = lax.dot_general(qh, kc, (((1,), (1,)), ((), ())), preferred_element_type=jnp.float32)
            if c == 0:
                s = jnp.where(seen, s, LOW)
            s_scr[:, c * CHUNK:(c + 1) * CHUNK] = s
            top = jnp.maximum(top, jnp.maximum(s[:, :HD], s[:, HD:]))
        top = jnp.broadcast_to(jnp.max(top, axis=1, keepdims=True), (TILE, HD))
        off = jnp.maximum(top, -1e20) * C2
        off = jnp.concatenate([off, off], axis=1)
        acc = None
        for c in range(KEYS // CHUNK):
            p = jnp.exp2(s_scr[:, c * CHUNK:(c + 1) * CHUNK] * C2 - off).astype(jnp.bfloat16)
            d = lax.dot_general(p, v_scr[pl.ds(c * CHUNK, CHUNK), h * HD:(h + 2) * HD],
                                (((1,), (0,)), ((), ())), preferred_element_type=jnp.float32)
            acc = d if acc is None else acc + d
        main, total = (acc[:, :HD], acc[:, HD:]) if h == 0 else (acc[:, HD:], acc[:, :HD])
        total = jnp.maximum(total, 1e-30)
        out_ref[:, 0:ROWS, h * HD:(h + 1) * HD] = (main / total).astype(jnp.bfloat16).reshape(
            SHARDS, ROWS, HD)
        stat = jnp.where(top > 0.5 * LOW, top * SCALE + jnp.log(total), LOW)
        coded.append([code_stat(stat[j * ROWS:(j + 1) * ROWS]) for j in range(SHARDS)])
    for j in range(SHARDS):
        out_ref[j, ROWS:, 0:ROWS] = jnp.concatenate([coded[0][j], coded[1][j]], axis=0).astype(jnp.bfloat16)
        out_ref[j, ROWS:, ROWS:] = jnp.zeros((STAT_ROWS, WIDTH - ROWS), jnp.bfloat16)


def partial_attention(place, q_all, pieces):
    return pl.pallas_call(
        partial_kernel,
        out_shape=jax.ShapeDtypeStruct((NY, ROWS + STAT_ROWS, WIDTH), jnp.bfloat16),
        grid=(NY // SHARDS,),
        in_specs=[IN_SMEM, pl.BlockSpec((SHARDS, ROWS, WIDTH), lambda i: (i, 0, 0))] + [ANY] * PIECES,
        out_specs=pl.BlockSpec((SHARDS, ROWS + STAT_ROWS, WIDTH), lambda i: (i, 0, 0)),
        scratch_shapes=[
            pltpu.VMEM((KEYS, 3 * HD), jnp.bfloat16),
            pltpu.VMEM((KEYS, 3 * HD), jnp.bfloat16),
            pltpu.VMEM((TILE, KEYS), jnp.float32),
            pltpu.SemaphoreType.DMA((PIECES, 4)),
        ],
        cost_estimate=pl.CostEstimate(
            flops=4 * NY * ROWS * KEYS * WIDTH, bytes_accessed=4 * KEYS * WIDTH,
            transcendentals=2 * NY * ROWS * KEYS),
        compiler_params=pltpu.CompilerParams(vmem_limit_bytes=18 << 20),
        name="partial_attention",
    )(place, q_all, *pieces)


def combine_kernel(part_ref, out_ref):
    parts = [part_ref.at[j] for j in range(NY)]
    stats = []
    for h in range(2):
        rows = []
        for part in parts:
            b = part[pl.ds(ROWS, STAT_ROWS), :].astype(jnp.float32)[8 * h:8 * h + 8]
            rows.append(b[0:1] + b[1:2] + b[2:3])
        top = functools.reduce(jnp.maximum, rows)
        ws = [jnp.exp(r - top) for r in rows]
        inv = 1.0 / functools.reduce(jnp.add, ws)
        stats += [w * inv for w in ws]
    cols = jnp.transpose(jnp.concatenate(stats, axis=0))[0:ROWS]
    for h in range(2):
        acc = jnp.zeros((ROWS, HD), jnp.float32)
        for j, part in enumerate(parts):
            o = part[0:ROWS, h * HD:(h + 1) * HD].astype(jnp.float32)
            acc = acc + o * cols[:, h * NY + j:h * NY + j + 1]
        out_ref[:, h * HD:(h + 1) * HD] = acc.astype(jnp.bfloat16)


def combine(parts):
    return pl.pallas_call(
        combine_kernel,
        out_shape=jax.ShapeDtypeStruct((ROWS, WIDTH), jnp.bfloat16),
        in_specs=[IN_VMEM],
        out_specs=IN_VMEM,
        compiler_params=pltpu.CompilerParams(vmem_limit_bytes=8 << 20),
        name="combine",
    )(parts)


def split_kernel(place_ref, nkv_ref, twin_ref, *refs):
    outs, sem = refs[:HEADS - 1], refs[HEADS - 1]
    me = place_ref[3]
    copies = []
    for k in range(1, HEADS):
        at = pl.multiple_of((me ^ k) * GROUP_WIDTH, GROUP_WIDTH)
        near = pl.multiple_of(((me ^ k) & (HEADS - 1)) * GROUP_WIDTH, GROUP_WIDTH)
        copies.append(pltpu.make_async_copy(
            nkv_ref.at[0, :, pl.ds(at, GROUP_WIDTH)], outs[k - 1].at[0], sem.at[k - 1, 0]))
        copies.append(pltpu.make_async_copy(
            twin_ref.at[:, pl.ds(near, GROUP_WIDTH)], outs[k - 1].at[1], sem.at[k - 1, 1]))
    for c in copies:
        c.start()
    for c in copies:
        c.wait()


def split_groups(place, neighbour_kv, twin):
    piece = jax.ShapeDtypeStruct((2, BLOCK, GROUP_WIDTH), jnp.bfloat16)
    return pl.pallas_call(
        split_kernel,
        out_shape=[piece] * (HEADS - 1),
        in_specs=[IN_SMEM, ANY, ANY],
        out_specs=[IN_VMEM] * (HEADS - 1),
        scratch_shapes=[pltpu.SemaphoreType.DMA((HEADS - 1, 2))],
        compiler_params=pltpu.CompilerParams(vmem_limit_bytes=8 << 20),
        name="split_groups",
    )(place, neighbour_kv, twin)


def cross_kernel(place_ref, map_ref, q_ref, nkv_ref, twin_ref, *refs):
    pieces = refs[:HEADS - 1]
    out_ref, scr, sem = refs[HEADS - 1:]
    me = place_ref[3]
    at = pl.multiple_of(me * GROUP_WIDTH, GROUP_WIDTH)
    near = pl.multiple_of((me & (HEADS - 1)) * GROUP_WIDTH, GROUP_WIDTH)
    copies = [
        pltpu.make_async_copy(nkv_ref.at[0, :, pl.ds(at, GROUP_WIDTH)], scr.at[0], sem.at[0]),
        pltpu.make_async_copy(twin_ref.at[:, pl.ds(near, GROUP_WIDTH)], scr.at[1], sem.at[1]),
    ]
    for k in range(1, HEADS):
        copies.append(pltpu.make_async_copy(pieces[k - 1], scr.at[pl.ds(2 * k, 2)], sem.at[2 * k]))
    for c in copies:
        c.start()
    for c in copies:
        c.wait()
    for c in range(STRETCHES):
        flips = [map_ref[c, r] ^ me for r in range(2)]
        slots = [(f & (HEADS - 1)) * 2 + ((f >> 2) & 1) for f in flips]
        keep = place_ref[4] * STRETCHES + c > 0
        for h in range(2):
            qh = q_ref[c * STRETCH:(c + 1) * STRETCH, h * HD:(h + 1) * HD]
            s = [lax.dot_general(qh, scr[slot, :, h * HD:(h + 1) * HD], (((1,), (1,)), ((), ())),
                                 preferred_element_type=jnp.float32) for slot in slots]
            top = jnp.max(jnp.maximum(s[0], s[1]), axis=1, keepdims=True) * C2
            p = [jnp.exp2(a * C2 - top) for a in s]
            total = jnp.sum(p[0] + p[1], axis=1, keepdims=True)
            o = sum(lax.dot_general(a.astype(jnp.bfloat16), scr[slot, :, WIDTH + h * HD:WIDTH + (h + 1) * HD],
                                    (((1,), (0,)), ((), ())), preferred_element_type=jnp.float32)
                    for a, slot in zip(p, slots))
            out_ref[c * STRETCH:(c + 1) * STRETCH, h * HD:(h + 1) * HD] = jnp.where(
                keep, o / total, 0.0).astype(jnp.bfloat16)


def cross(place, neighbour_map, query_cross, neighbour_kv, twin, pieces):
    return pl.pallas_call(
        cross_kernel,
        out_shape=jax.ShapeDtypeStruct((ROWS, WIDTH), jnp.bfloat16),
        in_specs=[IN_SMEM, IN_SMEM, IN_VMEM, ANY, ANY] + [ANY] * (HEADS - 1),
        out_specs=IN_VMEM,
        scratch_shapes=[
            pltpu.VMEM((GROUPS, BLOCK, GROUP_WIDTH), jnp.bfloat16),
            pltpu.SemaphoreType.DMA((GROUPS,)),
        ],
        cost_estimate=pl.CostEstimate(
            flops=8 * ROWS * 2 * BLOCK * WIDTH, bytes_accessed=2 << 20, transcendentals=4 * ROWS * BLOCK),
        compiler_params=pltpu.CompilerParams(vmem_limit_bytes=8 << 20),
        name="cross_attention",
    )(place, neighbour_map, query_cross, neighbour_kv, twin, *pieces)


def pack_kernel(q_ref, k_ref, v_ref, kv_ref, copies_ref, scr, sem):
    loads = [pltpu.make_async_copy(ref, scr.at[pl.ds(i * ROWS, ROWS), :], sem.at[i])
             for i, ref in enumerate((k_ref, v_ref, q_ref))]
    for c in loads:
        c.start()
    loads[0].wait()
    loads[1].wait()
    stores = [pltpu.make_async_copy(scr.at[pl.ds(0, 2 * ROWS), :], kv_ref, sem.at[3])]
    stores[0].start()
    loads[2].wait()
    for j in range(NY):
        stores.append(pltpu.make_async_copy(
            scr.at[pl.ds(2 * ROWS, ROWS), :], copies_ref.at[j], sem.at[4 + j]))
        stores[-1].start()
    for c in stores:
        c.wait()


def pack(query, key, value):
    return pl.pallas_call(
        pack_kernel,
        out_shape=[jax.ShapeDtypeStruct((2 * ROWS, WIDTH), jnp.bfloat16),
                   jax.ShapeDtypeStruct((NY, ROWS, WIDTH), jnp.bfloat16)],
        in_specs=[pl.BlockSpec(memory_space=pltpu.HBM)] * 3,
        out_specs=[ANY] * 2,
        scratch_shapes=[
            pltpu.VMEM((3 * ROWS, WIDTH), jnp.bfloat16),
            pltpu.SemaphoreType.DMA((4 + NY,)),
        ],
        compiler_params=pltpu.CompilerParams(vmem_limit_bytes=4 << 20),
        name="pack",
    )(query, key, value)


def on_device(query_self, key_self, value_self, query_cross, neighbour_kv, neighbour_map):
    x, zh, y = lax.axis_index("x"), lax.axis_index("zh"), lax.axis_index("y")
    me = lax.axis_index(("sec", "head"))
    place = jnp.stack([x, zh, y, me, lax.axis_index(("x", "zh", "y"))]).astype(jnp.int32)

    kv, copies = pack(query_self, key_self, value_self)
    kvz = lax.ppermute(kv, "zh", [(0, 1), (1, 0)])
    pieces = [kv]
    for k in range(1, NX):
        pieces.append(lax.ppermute(kv, "x", [(a, a + k) for a in range(NX - k)]))
    pieces.append(kvz)
    for k in range(1, NX):
        pieces.append(lax.ppermute(kvz, "x", [(a, a + k) for a in range(NX - k)]))
    q_all = lax.all_to_all(copies, "y", 0, 0, tiled=True)

    half = HEADS * GROUP_WIDTH
    mine = lax.dynamic_slice(
        neighbour_kv[0], (0, (1 - lax.axis_index("sec")) * half), (BLOCK, half))
    twin = lax.ppermute(mine, "sec", [(0, 1), (1, 0)])
    outgoing = split_groups(place, neighbour_kv, twin)
    arrived = [lax.ppermute(outgoing[k - 1], "head", [(a, a ^ k) for a in range(HEADS)])
               for k in range(1, HEADS)]

    parts = partial_attention(place, q_all, pieces)
    cross_out = cross(place, neighbour_map, query_cross, neighbour_kv, twin, arrived)
    received = lax.all_to_all(parts, "y", 0, 0, tiled=True)
    self_out = combine(received)
    return (self_out, cross_out)


def solution(mesh):
    fine = Mesh(mesh.devices.reshape(2, NX, NZ, NY, 4), ("sec", "x", "zh", "y", "head"))
    rows, cols = ("x", "zh", "y"), ("sec", "head")
    return jax.shard_map(
        on_device,
        mesh=fine,
        in_specs=(
            P(rows, cols),
            P(rows, cols),
            P(rows, cols),
            P(rows, cols),
            P(("sec", "x", "zh", "y", "head"), None, None),
            P(rows, None),
        ),
        out_specs=(P(rows, cols), P(rows, cols)),
        check_vma=False,
    )
```

```python
import functools
import math

import jax
import jax.numpy as jnp
from jax import lax
from jax.experimental import pallas as pl
from jax.experimental.pallas import tpu as pltpu
from jax.sharding import Mesh
from jax.sharding import PartitionSpec as P

HD = 128
STRETCH = 64
NX, NZ, NY = 4, 2, 8
ROWS = 192
WIDTH = 256
STAT_ROWS = 16
PIECES = NX * NZ
KEYS = PIECES * ROWS
CHUNK = 256
BLOCK = 128
GROUPS = 8
HEADS = 4
GROUP_WIDTH = 512
STRETCHES = ROWS // STRETCH
LOW = -1e30
SCALE = 1.0 / math.sqrt(HD)
C2 = SCALE * math.log2(math.e)
SHARDS = 4
TILE = SHARDS * ROWS

ANY = pl.BlockSpec(memory_space=pl.ANY)
IN_SMEM = pl.BlockSpec(memory_space=pltpu.SMEM)
IN_VMEM = pl.BlockSpec(memory_space=pltpu.VMEM)


def code_stat(stat):
    row = jnp.transpose(stat)[0:STAT_ROWS // 2, :]
    hi = row.astype(jnp.bfloat16).astype(jnp.float32)
    mid = (row - hi).astype(jnp.bfloat16).astype(jnp.float32)
    low = row - hi - mid
    at = lax.broadcasted_iota(jnp.int32, row.shape, 0)
    return jnp.where(at == 0, hi, jnp.where(at == 1, mid, low))


def partial_kernel(place_ref, q_ref, *refs):
    pieces, out_ref = refs[:PIECES], refs[PIECES]
    k_scr, v_scr, s_scr, sem = refs[PIECES + 1:]
    x, zh, y = place_ref[0], place_ref[1], place_ref[2]
    i = pl.program_id(0)

    @pl.when(i == 0)
    def _():
        copies = []
        for p in range(PIECES):
            kv, at = pieces[p], 0
            for h in range(2):
                copies.append(pltpu.make_async_copy(
                    kv.at[pl.ds(at, ROWS), pl.ds(h * HD, HD)],
                    k_scr.at[pl.ds(p * ROWS, ROWS), pl.ds(2 * h * HD, HD)], sem.at[p, h]))
                copies.append(pltpu.make_async_copy(
                    kv.at[pl.ds(at + ROWS, ROWS), pl.ds(h * HD, HD)],
                    v_scr.at[pl.ds(p * ROWS, ROWS), pl.ds(2 * h * HD, HD)], sem.at[p, 2 + h]))
        for c in copies:
            c.start()
        v_scr[:, HD:2 * HD] = jnp.ones((KEYS, HD), jnp.bfloat16)
        lane0 = lax.broadcasted_iota(jnp.int32, (ROWS, HD), 1) == 0
        for p in range(PIECES):
            hidden = jnp.logical_or(x < p // NZ, jnp.logical_and(zh == 0, p == 1))
            bias = jnp.where(hidden, LOW, 0.0)
            k_scr[pl.ds(p * ROWS, ROWS), HD:2 * HD] = jnp.where(lane0, bias, 0.0).astype(jnp.bfloat16)
        for c in copies:
            c.wait()

    one = jnp.where(lax.broadcasted_iota(jnp.int32, (TILE, HD), 1) == 0, 1.0, 0.0).astype(jnp.bfloat16)
    row = lax.broadcasted_iota(jnp.int32, (TILE, CHUNK), 0)
    col = lax.broadcasted_iota(jnp.int32, (TILE, CHUNK), 1)
    seen = jnp.logical_or(col >= ROWS, col - row <= i * TILE - y * ROWS)

    def attend(chunks):
        coded = []
        for h in range(2):
            qh = q_ref[:, :, h * HD:(h + 1) * HD].reshape(TILE, HD)
            qh = jnp.concatenate([qh, one] if h == 0 else [one, qh], axis=1)
            top = jnp.full((TILE, HD), LOW, jnp.float32)
            for c in range(chunks):
                kc = k_scr[pl.ds(c * CHUNK, CHUNK), h * HD:(h + 2) * HD]
                s = lax.dot_general(qh, kc, (((1,), (1,)), ((), ())), preferred_element_type=jnp.float32)
                if c == 0:
                    s = jnp.where(seen, s, LOW)
                s_scr[:, c * CHUNK:(c + 1) * CHUNK] = s
                top = jnp.maximum(top, jnp.maximum(s[:, :HD], s[:, HD:]))
            top = jnp.broadcast_to(jnp.max(top, axis=1, keepdims=True), (TILE, HD))
            off = jnp.maximum(top, -1e20) * C2
            off = jnp.concatenate([off, off], axis=1)
            acc = None
            for c in range(chunks):
                p = jnp.exp2(s_scr[:, c * CHUNK:(c + 1) * CHUNK] * C2 - off).astype(jnp.bfloat16)
                d = lax.dot_general(p, v_scr[pl.ds(c * CHUNK, CHUNK), h * HD:(h + 2) * HD],
                                    (((1,), (0,)), ((), ())), preferred_element_type=jnp.float32)
                acc = d if acc is None else acc + d
            main, total = (acc[:, :HD], acc[:, HD:]) if h == 0 else (acc[:, HD:], acc[:, :HD])
            total = jnp.maximum(total, 1e-30)
            out_ref[:, 0:ROWS, h * HD:(h + 1) * HD] = (main / total).astype(jnp.bfloat16).reshape(
                SHARDS, ROWS, HD)
            stat = jnp.where(top > 0.5 * LOW, top * SCALE + jnp.log(total), LOW)
            coded.append([code_stat(stat[j * ROWS:(j + 1) * ROWS]) for j in range(SHARDS)])
        for j in range(SHARDS):
            out_ref[j, ROWS:, 0:ROWS] = jnp.concatenate([coded[0][j], coded[1][j]], axis=0).astype(jnp.bfloat16)
            out_ref[j, ROWS:, ROWS:] = jnp.zeros((STAT_ROWS, WIDTH - ROWS), jnp.bfloat16)

    for rank in range(NX):
        @pl.when(x == rank)
        def _():
            attend(pl.cdiv((rank + 1) * NZ * ROWS, CHUNK))


def partial_attention(place, q_all, pieces):
    return pl.pallas_call(
        partial_kernel,
        out_shape=jax.ShapeDtypeStruct((NY, ROWS + STAT_ROWS, WIDTH), jnp.bfloat16),
        grid=(NY // SHARDS,),
        in_specs=[IN_SMEM, pl.BlockSpec((SHARDS, ROWS, WIDTH), lambda i: (i, 0, 0))] + [ANY] * PIECES,
        out_specs=pl.BlockSpec((SHARDS, ROWS + STAT_ROWS, WIDTH), lambda i: (i, 0, 0)),
        scratch_shapes=[
            pltpu.VMEM((KEYS, 3 * HD), jnp.bfloat16),
            pltpu.VMEM((KEYS, 3 * HD), jnp.bfloat16),
            pltpu.VMEM((TILE, KEYS), jnp.float32),
            pltpu.SemaphoreType.DMA((PIECES, 4)),
        ],
        cost_estimate=pl.CostEstimate(
            flops=4 * NY * ROWS * KEYS * WIDTH, bytes_accessed=4 * KEYS * WIDTH,
            transcendentals=2 * NY * ROWS * KEYS),
        compiler_params=pltpu.CompilerParams(vmem_limit_bytes=18 << 20),
        name="partial_attention",
    )(place, q_all, *pieces)


def combine_kernel(part_ref, out_ref):
    parts = [part_ref.at[j] for j in range(NY)]
    stats = []
    for h in range(2):
        rows = []
        for part in parts:
            b = part[pl.ds(ROWS, STAT_ROWS), :].astype(jnp.float32)[8 * h:8 * h + 8]
            rows.append(b[0:1] + b[1:2] + b[2:3])
        top = functools.reduce(jnp.maximum, rows)
        ws = [jnp.exp(r - top) for r in rows]
        inv = 1.0 / functools.reduce(jnp.add, ws)
        stats += [w * inv for w in ws]
    cols = jnp.transpose(jnp.concatenate(stats, axis=0))[0:ROWS]
    for h in range(2):
        acc = jnp.zeros((ROWS, HD), jnp.float32)
        for j, part in enumerate(parts):
            o = part[0:ROWS, h * HD:(h + 1) * HD].astype(jnp.float32)
            acc = acc + o * cols[:, h * NY + j:h * NY + j + 1]
        out_ref[:, h * HD:(h + 1) * HD] = acc.astype(jnp.bfloat16)


def combine(parts):
    return pl.pallas_call(
        combine_kernel,
        out_shape=jax.ShapeDtypeStruct((ROWS, WIDTH), jnp.bfloat16),
        in_specs=[IN_VMEM],
        out_specs=IN_VMEM,
        compiler_params=pltpu.CompilerParams(vmem_limit_bytes=8 << 20),
        name="combine",
    )(parts)


def split_kernel(place_ref, nkv_ref, twin_ref, *refs):
    outs, sem = refs[:HEADS - 1], refs[HEADS - 1]
    me = place_ref[3]
    copies = []
    for k in range(1, HEADS):
        at = pl.multiple_of((me ^ k) * GROUP_WIDTH, GROUP_WIDTH)
        near = pl.multiple_of(((me ^ k) & (HEADS - 1)) * GROUP_WIDTH, GROUP_WIDTH)
        copies.append(pltpu.make_async_copy(
            nkv_ref.at[0, :, pl.ds(at, GROUP_WIDTH)], outs[k - 1].at[0], sem.at[k - 1, 0]))
        copies.append(pltpu.make_async_copy(
            twin_ref.at[:, pl.ds(near, GROUP_WIDTH)], outs[k - 1].at[1], sem.at[k - 1, 1]))
    for c in copies:
        c.start()
    for c in copies:
        c.wait()


def split_groups(place, neighbour_kv, twin):
    piece = jax.ShapeDtypeStruct((2, BLOCK, GROUP_WIDTH), jnp.bfloat16)
    return pl.pallas_call(
        split_kernel,
        out_shape=[piece] * (HEADS - 1),
        in_specs=[IN_SMEM, ANY, ANY],
        out_specs=[IN_VMEM] * (HEADS - 1),
        scratch_shapes=[pltpu.SemaphoreType.DMA((HEADS - 1, 2))],
        compiler_params=pltpu.CompilerParams(vmem_limit_bytes=8 << 20),
        name="split_groups",
    )(place, neighbour_kv, twin)


def cross_kernel(place_ref, map_ref, q_ref, nkv_ref, twin_ref, *refs):
    pieces = refs[:HEADS - 1]
    out_ref, scr, sem = refs[HEADS - 1:]
    me = place_ref[3]
    at = pl.multiple_of(me * GROUP_WIDTH, GROUP_WIDTH)
    near = pl.multiple_of((me & (HEADS - 1)) * GROUP_WIDTH, GROUP_WIDTH)
    copies = [
        pltpu.make_async_copy(nkv_ref.at[0, :, pl.ds(at, GROUP_WIDTH)], scr.at[0], sem.at[0]),
        pltpu.make_async_copy(twin_ref.at[:, pl.ds(near, GROUP_WIDTH)], scr.at[1], sem.at[1]),
    ]
    for k in range(1, HEADS):
        copies.append(pltpu.make_async_copy(pieces[k - 1], scr.at[pl.ds(2 * k, 2)], sem.at[2 * k]))
    for c in copies:
        c.start()
    for c in copies:
        c.wait()
    for c in range(STRETCHES):
        flips = [map_ref[c, r] ^ me for r in range(2)]
        slots = [(f & (HEADS - 1)) * 2 + ((f >> 2) & 1) for f in flips]
        keep = place_ref[4] * STRETCHES + c > 0
        for h in range(2):
            qh = q_ref[c * STRETCH:(c + 1) * STRETCH, h * HD:(h + 1) * HD]
            s = [lax.dot_general(qh, scr[slot, :, h * HD:(h + 1) * HD], (((1,), (1,)), ((), ())),
                                 preferred_element_type=jnp.float32) for slot in slots]
            top = jnp.max(jnp.maximum(s[0], s[1]), axis=1, keepdims=True) * C2
            p = [jnp.exp2(a * C2 - top) for a in s]
            total = jnp.sum(p[0] + p[1], axis=1, keepdims=True)
            o = sum(lax.dot_general(a.astype(jnp.bfloat16), scr[slot, :, WIDTH + h * HD:WIDTH + (h + 1) * HD],
                                    (((1,), (0,)), ((), ())), preferred_element_type=jnp.float32)
                    for a, slot in zip(p, slots))
            out_ref[c * STRETCH:(c + 1) * STRETCH, h * HD:(h + 1) * HD] = jnp.where(
                keep, o / total, 0.0).astype(jnp.bfloat16)


def cross(place, neighbour_map, query_cross, neighbour_kv, twin, pieces):
    return pl.pallas_call(
        cross_kernel,
        out_shape=jax.ShapeDtypeStruct((ROWS, WIDTH), jnp.bfloat16),
        in_specs=[IN_SMEM, IN_SMEM, IN_VMEM, ANY, ANY] + [ANY] * (HEADS - 1),
        out_specs=IN_VMEM,
        scratch_shapes=[
            pltpu.VMEM((GROUPS, BLOCK, GROUP_WIDTH), jnp.bfloat16),
            pltpu.SemaphoreType.DMA((GROUPS,)),
        ],
        cost_estimate=pl.CostEstimate(
            flops=8 * ROWS * 2 * BLOCK * WIDTH, bytes_accessed=2 << 20, transcendentals=4 * ROWS * BLOCK),
        compiler_params=pltpu.CompilerParams(vmem_limit_bytes=8 << 20),
        name="cross_attention",
    )(place, neighbour_map, query_cross, neighbour_kv, twin, *pieces)


def on_device(query_self, key_self, value_self, query_cross, neighbour_kv, neighbour_map):
    x, zh, y = lax.axis_index("x"), lax.axis_index("zh"), lax.axis_index("y")
    me = lax.axis_index(("sec", "head"))
    place = jnp.stack([x, zh, y, me, lax.axis_index(("x", "zh", "y"))]).astype(jnp.int32)

    kv = jnp.concatenate([key_self, value_self], axis=0)
    kvz = lax.ppermute(kv, "zh", [(0, 1), (1, 0)])
    pieces = [kv, kvz]
    for k in range(1, NX):
        pairs = [(a, a + k) for a in range(NX - k)]
        pieces += [lax.ppermute(kv, "x", pairs), lax.ppermute(kvz, "x", pairs)]
    q_all = lax.all_to_all(
        jnp.broadcast_to(query_self[None], (NY, ROWS, WIDTH)), "y", 0, 0, tiled=True)

    half = HEADS * GROUP_WIDTH
    mine = lax.dynamic_slice(
        neighbour_kv[0], (0, (1 - lax.axis_index("sec")) * half), (BLOCK, half))
    twin = lax.ppermute(mine, "sec", [(0, 1), (1, 0)])
    outgoing = split_groups(place, neighbour_kv, twin)
    arrived = [lax.ppermute(outgoing[k - 1], "head", [(a, a ^ k) for a in range(HEADS)])
               for k in range(1, HEADS)]

    parts = partial_attention(place, q_all, pieces)
    cross_out = cross(place, neighbour_map, query_cross, neighbour_kv, twin, arrived)
    received = lax.all_to_all(parts, "y", 0, 0, tiled=True)
    self_out = combine(received)
    return (self_out, cross_out)


def solution(mesh):
    fine = Mesh(mesh.devices.reshape(2, NX, NZ, NY, 4), ("sec", "x", "zh", "y", "head"))
    rows, cols = ("x", "zh", "y"), ("sec", "head")
    return jax.shard_map(
        on_device,
        mesh=fine,
        in_specs=(
            P(rows, cols),
            P(rows, cols),
            P(rows, cols),
            P(rows, cols),
            P(("sec", "x", "zh", "y", "head"), None, None),
            P(rows, None),
        ),
        out_specs=(P(rows, cols), P(rows, cols)),
        check_vma=False,
    )
```

```python
import functools
import math

import jax
import jax.numpy as jnp
from jax import lax
from jax.experimental import pallas as pl
from jax.experimental.pallas import tpu as pltpu
from jax.sharding import Mesh
from jax.sharding import PartitionSpec as P

HD = 128
STRETCH = 64
NX, NZ, NY = 4, 2, 8
ROWS = 192
WIDTH = 256
STAT_ROWS = 16
PIECES = NX * NZ
KEYS = PIECES * ROWS
CHUNK = 256
BLOCK = 128
GROUPS = 8
HEADS = 4
GROUP_WIDTH = 512
STRETCHES = ROWS // STRETCH
LOW = -1e30
SCALE = 1.0 / math.sqrt(HD)
C2 = SCALE * math.log2(math.e)
SHARDS = 4
TILE = SHARDS * ROWS

ANY = pl.BlockSpec(memory_space=pl.ANY)
IN_SMEM = pl.BlockSpec(memory_space=pltpu.SMEM)
IN_VMEM = pl.BlockSpec(memory_space=pltpu.VMEM)


def partial_kernel(place_ref, q_ref, *refs):
    pieces, out_ref = refs[:PIECES], refs[PIECES]
    k_scr, v_scr, s_scr, sem = refs[PIECES + 1:]
    x, zh, y = place_ref[0], place_ref[1], place_ref[2]
    i = pl.program_id(0)

    def key_copies():
        return [pltpu.make_async_copy(
            pieces[p].at[pl.ds(0, ROWS), pl.ds(h * HD, HD)],
            k_scr.at[pl.ds(p * ROWS, ROWS), pl.ds(2 * h * HD, HD)], sem.at[p, h])
            for h in range(2) for p in range(PIECES)]

    def value_copies():
        return [pltpu.make_async_copy(
            pieces[p].at[pl.ds(ROWS, ROWS), pl.ds(h * HD, HD)],
            v_scr.at[pl.ds(p * ROWS, ROWS), pl.ds(2 * h * HD, HD)], sem.at[p, 2 + h])
            for h in range(2) for p in range(PIECES)]

    @pl.when(i == 0)
    def _():
        for c in key_copies() + value_copies():
            c.start()
        v_scr[:, HD:2 * HD] = jnp.ones((KEYS, HD), jnp.bfloat16)
        lane0 = lax.broadcasted_iota(jnp.int32, (ROWS, HD), 1) == 0
        for p in range(PIECES):
            hidden = jnp.logical_or(x < p // NZ, jnp.logical_and(zh == 0, p == 1))
            bias = jnp.where(hidden, LOW, 0.0)
            k_scr[pl.ds(p * ROWS, ROWS), HD:2 * HD] = jnp.where(lane0, bias, 0.0).astype(jnp.bfloat16)
        for c in key_copies():
            c.wait()

    one = jnp.where(lax.broadcasted_iota(jnp.int32, (TILE, HD), 1) == 0, 1.0, 0.0).astype(jnp.bfloat16)
    lane = lax.broadcasted_iota(jnp.int32, (ROWS, HD), 1)
    row = lax.broadcasted_iota(jnp.int32, (TILE, CHUNK), 0)
    col = lax.broadcasted_iota(jnp.int32, (TILE, CHUNK), 1)
    seen = jnp.logical_or(col >= ROWS, col - row <= i * TILE - y * ROWS)

    def attend(chunks):
        table = jnp.ones((ROWS, HD), jnp.float32)
        for h in range(2):
            qh = q_ref[:, :, h * HD:(h + 1) * HD].reshape(TILE, HD)
            qh = jnp.concatenate([qh, one] if h == 0 else [one, qh], axis=1)
            top = jnp.full((TILE, HD), LOW, jnp.float32)
            for c in range(chunks):
                kc = k_scr[pl.ds(c * CHUNK, CHUNK), h * HD:(h + 2) * HD]
                s = lax.dot_general(qh, kc, (((1,), (1,)), ((), ())), preferred_element_type=jnp.float32)
                if c == 0:
                    s = jnp.where(seen, s, LOW)
                s_scr[:, c * CHUNK:(c + 1) * CHUNK] = s
                top = jnp.maximum(top, jnp.maximum(s[:, :HD], s[:, HD:]))
            if h == 0:
                @pl.when(i == 0)
                def _():
                    for c in value_copies():
                        c.wait()
            top = jnp.broadcast_to(jnp.max(top, axis=1, keepdims=True), (TILE, HD))
            off = jnp.maximum(top, -1e20) * C2
            off = jnp.concatenate([off, off], axis=1)
            acc = None
            for c in range(chunks):
                p = jnp.exp2(s_scr[:, c * CHUNK:(c + 1) * CHUNK] * C2 - off).astype(jnp.bfloat16)
                d = lax.dot_general(p, v_scr[pl.ds(c * CHUNK, CHUNK), h * HD:(h + 2) * HD],
                                    (((1,), (0,)), ((), ())), preferred_element_type=jnp.float32)
                acc = d if acc is None else acc + d
            main, total = (acc[:, :HD], acc[:, HD:]) if h == 0 else (acc[:, HD:], acc[:, :HD])
            total = jnp.maximum(total, 1e-30)
            out_ref[:, 0:ROWS, h * HD:(h + 1) * HD] = (main / total).astype(jnp.bfloat16).reshape(
                SHARDS, ROWS, HD)
            for j in range(SHARDS):
                part = slice(j * ROWS, (j + 1) * ROWS)
                table = jnp.where(lane == 2 * j + h, top[part], table)
                table = jnp.where(lane == 2 * (SHARDS + j) + h, total[part], table)
        turned = jnp.transpose(table)
        tops, totals = turned[0:2 * SHARDS], turned[2 * SHARDS:4 * SHARDS]
        stat = jnp.where(tops > 0.5 * LOW, tops * SCALE + jnp.log(totals), LOW)
        hi = stat.astype(jnp.bfloat16).astype(jnp.float32)
        mid = (stat - hi).astype(jnp.bfloat16).astype(jnp.float32)
        low = stat - hi - mid
        at = lax.broadcasted_iota(jnp.int32, (STAT_ROWS // 2, ROWS), 0)
        for j in range(SHARDS):
            rows = []
            for r in (2 * j, 2 * j + 1):
                rows.append(jnp.where(at == 0, hi[r:r + 1], jnp.where(at == 1, mid[r:r + 1], low[r:r + 1])))
            out_ref[j, ROWS:, 0:ROWS] = jnp.concatenate(rows, axis=0).astype(jnp.bfloat16)
            out_ref[j, ROWS:, ROWS:] = jnp.zeros((STAT_ROWS, WIDTH - ROWS), jnp.bfloat16)

    for rank in range(NX):
        @pl.when(x == rank)
        def _():
            attend(pl.cdiv((rank + 1) * NZ * ROWS, CHUNK))


def partial_attention(place, q_all, pieces):
    return pl.pallas_call(
        partial_kernel,
        out_shape=jax.ShapeDtypeStruct((NY, ROWS + STAT_ROWS, WIDTH), jnp.bfloat16),
        grid=(NY // SHARDS,),
        in_specs=[IN_SMEM, pl.BlockSpec((SHARDS, ROWS, WIDTH), lambda i: (i, 0, 0))] + [ANY] * PIECES,
        out_specs=pl.BlockSpec((SHARDS, ROWS + STAT_ROWS, WIDTH), lambda i: (i, 0, 0)),
        scratch_shapes=[
            pltpu.VMEM((KEYS, 3 * HD), jnp.bfloat16),
            pltpu.VMEM((KEYS, 3 * HD), jnp.bfloat16),
            pltpu.VMEM((TILE, KEYS), jnp.float32),
            pltpu.SemaphoreType.DMA((PIECES, 4)),
        ],
        cost_estimate=pl.CostEstimate(
            flops=4 * NY * ROWS * KEYS * WIDTH, bytes_accessed=4 * KEYS * WIDTH,
            transcendentals=2 * NY * ROWS * KEYS),
        compiler_params=pltpu.CompilerParams(vmem_limit_bytes=18 << 20),
        name="partial_attention",
    )(place, q_all, *pieces)


def combine_kernel(part_ref, out_ref):
    parts = [part_ref.at[j] for j in range(NY)]
    stats = []
    for h in range(2):
        rows = []
        for part in parts:
            b = part[pl.ds(ROWS, STAT_ROWS), :].astype(jnp.float32)[8 * h:8 * h + 8]
            rows.append(b[0:1] + b[1:2] + b[2:3])
        top = functools.reduce(jnp.maximum, rows)
        ws = [jnp.exp(r - top) for r in rows]
        inv = 1.0 / functools.reduce(jnp.add, ws)
        stats += [w * inv for w in ws]
    cols = jnp.transpose(jnp.concatenate(stats, axis=0))[0:ROWS]
    for h in range(2):
        acc = jnp.zeros((ROWS, HD), jnp.float32)
        for j, part in enumerate(parts):
            o = part[0:ROWS, h * HD:(h + 1) * HD].astype(jnp.float32)
            acc = acc + o * cols[:, h * NY + j:h * NY + j + 1]
        out_ref[:, h * HD:(h + 1) * HD] = acc.astype(jnp.bfloat16)


def combine(parts):
    return pl.pallas_call(
        combine_kernel,
        out_shape=jax.ShapeDtypeStruct((ROWS, WIDTH), jnp.bfloat16),
        in_specs=[IN_VMEM],
        out_specs=IN_VMEM,
        compiler_params=pltpu.CompilerParams(vmem_limit_bytes=8 << 20),
        name="combine",
    )(parts)


def split_kernel(place_ref, nkv_ref, twin_ref, *refs):
    outs, sem = refs[:HEADS - 1], refs[HEADS - 1]
    me = place_ref[3]
    copies = []
    for k in range(1, HEADS):
        at = pl.multiple_of((me ^ k) * GROUP_WIDTH, GROUP_WIDTH)
        near = pl.multiple_of(((me ^ k) & (HEADS - 1)) * GROUP_WIDTH, GROUP_WIDTH)
        copies.append(pltpu.make_async_copy(
            nkv_ref.at[0, :, pl.ds(at, GROUP_WIDTH)], outs[k - 1].at[0], sem.at[k - 1, 0]))
        copies.append(pltpu.make_async_copy(
            twin_ref.at[:, pl.ds(near, GROUP_WIDTH)], outs[k - 1].at[1], sem.at[k - 1, 1]))
    for c in copies:
        c.start()
    for c in copies:
        c.wait()


def split_groups(place, neighbour_kv, twin):
    piece = jax.ShapeDtypeStruct((2, BLOCK, GROUP_WIDTH), jnp.bfloat16)
    return pl.pallas_call(
        split_kernel,
        out_shape=[piece] * (HEADS - 1),
        in_specs=[IN_SMEM, ANY, ANY],
        out_specs=[IN_VMEM] * (HEADS - 1),
        scratch_shapes=[pltpu.SemaphoreType.DMA((HEADS - 1, 2))],
        compiler_params=pltpu.CompilerParams(vmem_limit_bytes=8 << 20),
        name="split_groups",
    )(place, neighbour_kv, twin)


def cross_kernel(place_ref, map_ref, q_ref, nkv_ref, twin_ref, *refs):
    pieces = refs[:HEADS - 1]
    out_ref, scr, sem = refs[HEADS - 1:]
    me = place_ref[3]
    at = pl.multiple_of(me * GROUP_WIDTH, GROUP_WIDTH)
    near = pl.multiple_of((me & (HEADS - 1)) * GROUP_WIDTH, GROUP_WIDTH)
    copies = [
        pltpu.make_async_copy(nkv_ref.at[0, :, pl.ds(at, GROUP_WIDTH)], scr.at[0], sem.at[0]),
        pltpu.make_async_copy(twin_ref.at[:, pl.ds(near, GROUP_WIDTH)], scr.at[1], sem.at[1]),
    ]
    for k in range(1, HEADS):
        copies.append(pltpu.make_async_copy(pieces[k - 1], scr.at[pl.ds(2 * k, 2)], sem.at[2 * k]))
    for c in copies:
        c.start()
    for c in copies:
        c.wait()
    for c in range(STRETCHES):
        flips = [map_ref[c, r] ^ me for r in range(2)]
        slots = [(f & (HEADS - 1)) * 2 + ((f >> 2) & 1) for f in flips]
        keep = place_ref[4] * STRETCHES + c > 0
        for h in range(2):
            qh = q_ref[c * STRETCH:(c + 1) * STRETCH, h * HD:(h + 1) * HD]
            s = [lax.dot_general(qh, scr[slot, :, h * HD:(h + 1) * HD], (((1,), (1,)), ((), ())),
                                 preferred_element_type=jnp.float32) for slot in slots]
            top = jnp.max(jnp.maximum(s[0], s[1]), axis=1, keepdims=True) * C2
            p = [jnp.exp2(a * C2 - top) for a in s]
            total = jnp.sum(p[0] + p[1], axis=1, keepdims=True)
            o = sum(lax.dot_general(a.astype(jnp.bfloat16), scr[slot, :, WIDTH + h * HD:WIDTH + (h + 1) * HD],
                                    (((1,), (0,)), ((), ())), preferred_element_type=jnp.float32)
                    for a, slot in zip(p, slots))
            out_ref[c * STRETCH:(c + 1) * STRETCH, h * HD:(h + 1) * HD] = jnp.where(
                keep, o / total, 0.0).astype(jnp.bfloat16)


def cross(place, neighbour_map, query_cross, neighbour_kv, twin, pieces):
    return pl.pallas_call(
        cross_kernel,
        out_shape=jax.ShapeDtypeStruct((ROWS, WIDTH), jnp.bfloat16),
        in_specs=[IN_SMEM, IN_SMEM, IN_VMEM, ANY, ANY] + [ANY] * (HEADS - 1),
        out_specs=IN_VMEM,
        scratch_shapes=[
            pltpu.VMEM((GROUPS, BLOCK, GROUP_WIDTH), jnp.bfloat16),
            pltpu.SemaphoreType.DMA((GROUPS,)),
        ],
        cost_estimate=pl.CostEstimate(
            flops=8 * ROWS * 2 * BLOCK * WIDTH, bytes_accessed=2 << 20, transcendentals=4 * ROWS * BLOCK),
        compiler_params=pltpu.CompilerParams(vmem_limit_bytes=8 << 20),
        name="cross_attention",
    )(place, neighbour_map, query_cross, neighbour_kv, twin, *pieces)


def on_device(query_self, key_self, value_self, query_cross, neighbour_kv, neighbour_map):
    x, zh, y = lax.axis_index("x"), lax.axis_index("zh"), lax.axis_index("y")
    me = lax.axis_index(("sec", "head"))
    place = jnp.stack([x, zh, y, me, lax.axis_index(("x", "zh", "y"))]).astype(jnp.int32)

    kv = jnp.concatenate([key_self, value_self], axis=0)
    kvz = lax.ppermute(kv, "zh", [(0, 1), (1, 0)])
    pieces = [kv, kvz]
    for k in range(1, NX):
        pairs = [(a, a + k) for a in range(NX - k)]
        pieces += [lax.ppermute(kv, "x", pairs), lax.ppermute(kvz, "x", pairs)]
    q_all = lax.all_to_all(
        jnp.broadcast_to(query_self[None], (NY, ROWS, WIDTH)), "y", 0, 0, tiled=True)

    half = HEADS * GROUP_WIDTH
    mine = lax.dynamic_slice(
        neighbour_kv[0], (0, (1 - lax.axis_index("sec")) * half), (BLOCK, half))
    twin = lax.ppermute(mine, "sec", [(0, 1), (1, 0)])
    outgoing = split_groups(place, neighbour_kv, twin)
    arrived = [lax.ppermute(outgoing[k - 1], "head", [(a, a ^ k) for a in range(HEADS)])
               for k in range(1, HEADS)]

    parts = partial_attention(place, q_all, pieces)
    cross_out = cross(place, neighbour_map, query_cross, neighbour_kv, twin, arrived)
    received = lax.all_to_all(parts, "y", 0, 0, tiled=True)
    self_out = combine(received)
    return (self_out, cross_out)


def solution(mesh):
    fine = Mesh(mesh.devices.reshape(2, NX, NZ, NY, 4), ("sec", "x", "zh", "y", "head"))
    rows, cols = ("x", "zh", "y"), ("sec", "head")
    return jax.shard_map(
        on_device,
        mesh=fine,
        in_specs=(
            P(rows, cols),
            P(rows, cols),
            P(rows, cols),
            P(rows, cols),
            P(("sec", "x", "zh", "y", "head"), None, None),
            P(rows, None),
        ),
        out_specs=(P(rows, cols), P(rows, cols)),
        check_vma=False,
    )
```

```python
import functools
import math

import jax
import jax.numpy as jnp
from jax import lax
from jax.experimental import pallas as pl
from jax.experimental.pallas import tpu as pltpu
from jax.sharding import Mesh
from jax.sharding import PartitionSpec as P

HD = 128
STRETCH = 64
NX, NZ, NY = 4, 2, 8
ROWS = 192
WIDTH = 256
STAT_ROWS = 16
PIECES = NX * NZ
KEYS = PIECES * ROWS
CHUNK = 256
BLOCK = 128
GROUPS = 8
HEADS = 4
GROUP_WIDTH = 512
STRETCHES = ROWS // STRETCH
LOW = -1e30
SCALE = 1.0 / math.sqrt(HD)
C2 = SCALE * math.log2(math.e)
SHARDS = 4
TILE = SHARDS * ROWS

ANY = pl.BlockSpec(memory_space=pl.ANY)
IN_SMEM = pl.BlockSpec(memory_space=pltpu.SMEM)
IN_VMEM = pl.BlockSpec(memory_space=pltpu.VMEM)


def partial_kernel(place_ref, q_ref, *refs):
    pieces, out_ref = refs[:PIECES], refs[PIECES]
    bias_scr, s_scr = refs[PIECES + 1:]
    x, zh, y = place_ref[0], place_ref[1], place_ref[2]
    i = pl.program_id(0)

    @pl.when(i == 0)
    def _():
        lane0 = lax.broadcasted_iota(jnp.int32, (ROWS, HD), 1) == 0
        for p in range(PIECES):
            hidden = jnp.logical_or(x < p // NZ, jnp.logical_and(zh == 0, p == 1))
            bias = jnp.where(hidden, LOW, 0.0)
            bias_scr[pl.ds(p * ROWS, ROWS), :] = jnp.where(lane0, bias, 0.0).astype(jnp.bfloat16)

    def rows_of(c, h, base):
        parts, at = [], c * CHUNK
        while at < (c + 1) * CHUNK:
            p, r = divmod(at, ROWS)
            n = min(ROWS - r, (c + 1) * CHUNK - at)
            parts.append(pieces[p][base + r:base + r + n, h * HD:(h + 1) * HD])
            at += n
        return jnp.concatenate(parts, axis=0)

    ones = jnp.ones((CHUNK, HD), jnp.bfloat16)
    one = jnp.where(lax.broadcasted_iota(jnp.int32, (TILE, HD), 1) == 0, 1.0, 0.0).astype(jnp.bfloat16)
    lane = lax.broadcasted_iota(jnp.int32, (ROWS, HD), 1)
    row = lax.broadcasted_iota(jnp.int32, (TILE, CHUNK), 0)
    col = lax.broadcasted_iota(jnp.int32, (TILE, CHUNK), 1)
    seen = jnp.logical_or(col >= ROWS, col - row <= i * TILE - y * ROWS)

    def attend(chunks):
        table = jnp.ones((ROWS, HD), jnp.float32)
        for h in range(2):
            qh = q_ref[:, :, h * HD:(h + 1) * HD].reshape(TILE, HD)
            qh = jnp.concatenate([qh, one], axis=1)
            top = jnp.full((TILE, HD), LOW, jnp.float32)
            for c in range(chunks):
                kc = jnp.concatenate([rows_of(c, h, 0), bias_scr[pl.ds(c * CHUNK, CHUNK), :]], axis=1)
                s = lax.dot_general(qh, kc, (((1,), (1,)), ((), ())), preferred_element_type=jnp.float32)
                if c == 0:
                    s = jnp.where(seen, s, LOW)
                s_scr[:, c * CHUNK:(c + 1) * CHUNK] = s
                top = jnp.maximum(top, jnp.maximum(s[:, :HD], s[:, HD:]))
            top = jnp.broadcast_to(jnp.max(top, axis=1, keepdims=True), (TILE, HD))
            off = jnp.maximum(top, -1e20) * C2
            off = jnp.concatenate([off, off], axis=1)
            acc = None
            for c in range(chunks):
                p = jnp.exp2(s_scr[:, c * CHUNK:(c + 1) * CHUNK] * C2 - off).astype(jnp.bfloat16)
                vc = jnp.concatenate([rows_of(c, h, ROWS), ones], axis=1)
                d = lax.dot_general(p, vc, (((1,), (0,)), ((), ())), preferred_element_type=jnp.float32)
                acc = d if acc is None else acc + d
            main, total = acc[:, :HD], jnp.maximum(acc[:, HD:], 1e-30)
            out_ref[:, 0:ROWS, h * HD:(h + 1) * HD] = (main / total).astype(jnp.bfloat16).reshape(
                SHARDS, ROWS, HD)
            for j in range(SHARDS):
                part = slice(j * ROWS, (j + 1) * ROWS)
                table = jnp.where(lane == 2 * j + h, top[part], table)
                table = jnp.where(lane == 2 * (SHARDS + j) + h, total[part], table)
        turned = jnp.transpose(table)
        tops, totals = turned[0:2 * SHARDS], turned[2 * SHARDS:4 * SHARDS]
        stat = jnp.where(tops > 0.5 * LOW, tops * SCALE + jnp.log(totals), LOW)
        hi = stat.astype(jnp.bfloat16).astype(jnp.float32)
        mid = (stat - hi).astype(jnp.bfloat16).astype(jnp.float32)
        low = stat - hi - mid
        at = lax.broadcasted_iota(jnp.int32, (STAT_ROWS // 2, ROWS), 0)
        for j in range(SHARDS):
            rows = []
            for r in (2 * j, 2 * j + 1):
                rows.append(jnp.where(at == 0, hi[r:r + 1], jnp.where(at == 1, mid[r:r + 1], low[r:r + 1])))
            out_ref[j, ROWS:, 0:ROWS] = jnp.concatenate(rows, axis=0).astype(jnp.bfloat16)
            out_ref[j, ROWS:, ROWS:] = jnp.zeros((STAT_ROWS, WIDTH - ROWS), jnp.bfloat16)

    for rank in range(NX):
        @pl.when(x == rank)
        def _():
            attend(pl.cdiv((rank + 1) * NZ * ROWS, CHUNK))


def partial_attention(place, q_all, pieces):
    return pl.pallas_call(
        partial_kernel,
        out_shape=jax.ShapeDtypeStruct((NY, ROWS + STAT_ROWS, WIDTH), jnp.bfloat16),
        grid=(NY // SHARDS,),
        in_specs=[IN_SMEM, pl.BlockSpec((SHARDS, ROWS, WIDTH), lambda i: (i, 0, 0))] + [IN_VMEM] * PIECES,
        out_specs=pl.BlockSpec((SHARDS, ROWS + STAT_ROWS, WIDTH), lambda i: (i, 0, 0)),
        scratch_shapes=[
            pltpu.VMEM((KEYS, HD), jnp.bfloat16),
            pltpu.VMEM((TILE, KEYS), jnp.float32),
        ],
        cost_estimate=pl.CostEstimate(
            flops=4 * NY * ROWS * KEYS * WIDTH, bytes_accessed=4 * KEYS * WIDTH,
            transcendentals=2 * NY * ROWS * KEYS),
        compiler_params=pltpu.CompilerParams(vmem_limit_bytes=18 << 20),
        name="partial_attention",
    )(place, q_all, *pieces)


def combine_kernel(part_ref, out_ref):
    parts = [part_ref.at[j] for j in range(NY)]
    stats = []
    for h in range(2):
        rows = []
        for part in parts:
            b = part[pl.ds(ROWS, STAT_ROWS), :].astype(jnp.float32)[8 * h:8 * h + 8]
            rows.append(b[0:1] + b[1:2] + b[2:3])
        top = functools.reduce(jnp.maximum, rows)
        ws = [jnp.exp(r - top) for r in rows]
        inv = 1.0 / functools.reduce(jnp.add, ws)
        stats += [w * inv for w in ws]
    cols = jnp.transpose(jnp.concatenate(stats, axis=0))[0:ROWS]
    for h in range(2):
        acc = jnp.zeros((ROWS, HD), jnp.float32)
        for j, part in enumerate(parts):
            o = part[0:ROWS, h * HD:(h + 1) * HD].astype(jnp.float32)
            acc = acc + o * cols[:, h * NY + j:h * NY + j + 1]
        out_ref[:, h * HD:(h + 1) * HD] = acc.astype(jnp.bfloat16)


def combine(parts):
    return pl.pallas_call(
        combine_kernel,
        out_shape=jax.ShapeDtypeStruct((ROWS, WIDTH), jnp.bfloat16),
        in_specs=[IN_VMEM],
        out_specs=IN_VMEM,
        compiler_params=pltpu.CompilerParams(vmem_limit_bytes=8 << 20),
        name="combine",
    )(parts)


def split_kernel(place_ref, nkv_ref, twin_ref, *refs):
    outs, sem = refs[:HEADS - 1], refs[HEADS - 1]
    me = place_ref[3]
    copies = []
    for k in range(1, HEADS):
        at = pl.multiple_of((me ^ k) * GROUP_WIDTH, GROUP_WIDTH)
        near = pl.multiple_of(((me ^ k) & (HEADS - 1)) * GROUP_WIDTH, GROUP_WIDTH)
        copies.append(pltpu.make_async_copy(
            nkv_ref.at[0, :, pl.ds(at, GROUP_WIDTH)], outs[k - 1].at[0], sem.at[k - 1, 0]))
        copies.append(pltpu.make_async_copy(
            twin_ref.at[:, pl.ds(near, GROUP_WIDTH)], outs[k - 1].at[1], sem.at[k - 1, 1]))
    for c in copies:
        c.start()
    for c in copies:
        c.wait()


def split_groups(place, neighbour_kv, twin):
    piece = jax.ShapeDtypeStruct((2, BLOCK, GROUP_WIDTH), jnp.bfloat16)
    return pl.pallas_call(
        split_kernel,
        out_shape=[piece] * (HEADS - 1),
        in_specs=[IN_SMEM, ANY, ANY],
        out_specs=[IN_VMEM] * (HEADS - 1),
        scratch_shapes=[pltpu.SemaphoreType.DMA((HEADS - 1, 2))],
        compiler_params=pltpu.CompilerParams(vmem_limit_bytes=8 << 20),
        name="split_groups",
    )(place, neighbour_kv, twin)


def cross_kernel(place_ref, map_ref, q_ref, nkv_ref, twin_ref, *refs):
    pieces = refs[:HEADS - 1]
    out_ref, scr, sem = refs[HEADS - 1:]
    me = place_ref[3]
    at = pl.multiple_of(me * GROUP_WIDTH, GROUP_WIDTH)
    near = pl.multiple_of((me & (HEADS - 1)) * GROUP_WIDTH, GROUP_WIDTH)
    copies = [
        pltpu.make_async_copy(nkv_ref.at[0, :, pl.ds(at, GROUP_WIDTH)], scr.at[0], sem.at[0]),
        pltpu.make_async_copy(twin_ref.at[:, pl.ds(near, GROUP_WIDTH)], scr.at[1], sem.at[1]),
    ]
    for k in range(1, HEADS):
        copies.append(pltpu.make_async_copy(pieces[k - 1], scr.at[pl.ds(2 * k, 2)], sem.at[2 * k]))
    for c in copies:
        c.start()
    for c in copies:
        c.wait()
    for c in range(STRETCHES):
        flips = [map_ref[c, r] ^ me for r in range(2)]
        slots = [(f & (HEADS - 1)) * 2 + ((f >> 2) & 1) for f in flips]
        keep = place_ref[4] * STRETCHES + c > 0
        for h in range(2):
            qh = q_ref[c * STRETCH:(c + 1) * STRETCH, h * HD:(h + 1) * HD]
            s = [lax.dot_general(qh, scr[slot, :, h * HD:(h + 1) * HD], (((1,), (1,)), ((), ())),
                                 preferred_element_type=jnp.float32) for slot in slots]
            top = jnp.max(jnp.maximum(s[0], s[1]), axis=1, keepdims=True) * C2
            p = [jnp.exp2(a * C2 - top) for a in s]
            total = jnp.sum(p[0] + p[1], axis=1, keepdims=True)
            o = sum(lax.dot_general(a.astype(jnp.bfloat16), scr[slot, :, WIDTH + h * HD:WIDTH + (h + 1) * HD],
                                    (((1,), (0,)), ((), ())), preferred_element_type=jnp.float32)
                    for a, slot in zip(p, slots))
            out_ref[c * STRETCH:(c + 1) * STRETCH, h * HD:(h + 1) * HD] = jnp.where(
                keep, o / total, 0.0).astype(jnp.bfloat16)


def cross(place, neighbour_map, query_cross, neighbour_kv, twin, pieces):
    return pl.pallas_call(
        cross_kernel,
        out_shape=jax.ShapeDtypeStruct((ROWS, WIDTH), jnp.bfloat16),
        in_specs=[IN_SMEM, IN_SMEM, IN_VMEM, ANY, ANY] + [ANY] * (HEADS - 1),
        out_specs=IN_VMEM,
        scratch_shapes=[
            pltpu.VMEM((GROUPS, BLOCK, GROUP_WIDTH), jnp.bfloat16),
            pltpu.SemaphoreType.DMA((GROUPS,)),
        ],
        cost_estimate=pl.CostEstimate(
            flops=8 * ROWS * 2 * BLOCK * WIDTH, bytes_accessed=2 << 20, transcendentals=4 * ROWS * BLOCK),
        compiler_params=pltpu.CompilerParams(vmem_limit_bytes=8 << 20),
        name="cross_attention",
    )(place, neighbour_map, query_cross, neighbour_kv, twin, *pieces)


def on_device(query_self, key_self, value_self, query_cross, neighbour_kv, neighbour_map):
    x, zh, y = lax.axis_index("x"), lax.axis_index("zh"), lax.axis_index("y")
    me = lax.axis_index(("sec", "head"))
    place = jnp.stack([x, zh, y, me, lax.axis_index(("x", "zh", "y"))]).astype(jnp.int32)

    kv = jnp.concatenate([key_self, value_self], axis=0)
    kvz = lax.ppermute(kv, "zh", [(0, 1), (1, 0)])
    pieces = [kv, kvz]
    for k in range(1, NX):
        pairs = [(a, a + k) for a in range(NX - k)]
        pieces += [lax.ppermute(kv, "x", pairs), lax.ppermute(kvz, "x", pairs)]
    q_all = lax.all_to_all(
        jnp.broadcast_to(query_self[None], (NY, ROWS, WIDTH)), "y", 0, 0, tiled=True)

    half = HEADS * GROUP_WIDTH
    mine = lax.dynamic_slice(
        neighbour_kv[0], (0, (1 - lax.axis_index("sec")) * half), (BLOCK, half))
    twin = lax.ppermute(mine, "sec", [(0, 1), (1, 0)])
    outgoing = split_groups(place, neighbour_kv, twin)
    arrived = [lax.ppermute(outgoing[k - 1], "head", [(a, a ^ k) for a in range(HEADS)])
               for k in range(1, HEADS)]

    parts = partial_attention(place, q_all, pieces)
    cross_out = cross(place, neighbour_map, query_cross, neighbour_kv, twin, arrived)
    received = lax.all_to_all(parts, "y", 0, 0, tiled=True)
    self_out = combine(received)
    return (self_out, cross_out)


def solution(mesh):
    fine = Mesh(mesh.devices.reshape(2, NX, NZ, NY, 4), ("sec", "x", "zh", "y", "head"))
    rows, cols = ("x", "zh", "y"), ("sec", "head")
    return jax.shard_map(
        on_device,
        mesh=fine,
        in_specs=(
            P(rows, cols),
            P(rows, cols),
            P(rows, cols),
            P(rows, cols),
            P(("sec", "x", "zh", "y", "head"), None, None),
            P(rows, None),
        ),
        out_specs=(P(rows, cols), P(rows, cols)),
        check_vma=False,
    )
```
